256 devices in a mesh: ctx: 32 (over z, y_lo, core), tp: 8 (over y_hi, x).
Axes of the slice: x: 4, y: 4 (y_hi: 2, y_lo: 2; y = y_hi * 2 + y_lo), z: 8, core: 2. Of those that a mesh axis runs over, the one named last changes fastest.
Arguments:
- proj: bfloat16 [16384, 3, 4096], P('ctx', None, 'tp'), may hold values from -6 to 6
- short_filter: float32 [3, 3, 4096], P(None, None, 'tp'), may hold values from -3 to 3
- long_filter: float32 [16384, 4096], P(None, ('tp', 'ctx')), may hold values from -1 to 2.5
- out_weight: bfloat16 [4096, 4096], P('tp'), may hold values from -0.125 to 0.125
Outputs:
- block_out: bfloat16 [16384, 4096], P('ctx', 'tp')
The draws below stay inside these ranges and needn't reach their ends.
All inputs are finite; a program needn't handle non-finite values.
Results may differ from the reference program's by a relative error of at most 0.0064.
Values may be sent and summed in bfloat16 or wider, within the bound.
No kernel may reach another device: no remote copies, remote signals or barrier semaphores. Data moves between devices by JAX's collectives and lax.ppermute only.
A program may use at most 64 MiB of HBM per device.

```python
import math
import jax
import jax.numpy as jnp
from jax import lax

MODEL_WIDTH = 4096
TAPS = 3
SEQUENCE_TOKENS = 16384


def draw_long_filter(key, part):
    random_subkeys = jax.random.split(key, 5)
    token_positions = jnp.arange(SEQUENCE_TOKENS, dtype=jnp.float32)[:, None]
    decay_len = jnp.exp(jax.random.uniform(random_subkeys[0], (1, MODEL_WIDTH), jnp.float32, jnp.log(32.0), jnp.log(4.0 * SEQUENCE_TOKENS)))
    rough_part = jnp.clip(jax.random.normal(random_subkeys[1], (SEQUENCE_TOKENS, MODEL_WIDTH), jnp.float32), -4.0, 4.0)
    direct = jax.random.uniform(random_subkeys[2], (1, MODEL_WIDTH), jnp.float32, 0.5, 1.5)
    spike_position = jax.random.randint(random_subkeys[3], (4,), 1, SEQUENCE_TOKENS).astype(jnp.float32)
    spike_decrease = jax.random.uniform(random_subkeys[4], (4, MODEL_WIDTH), jnp.float32, jnp.log(0.5), jnp.log(0.8))
    log_multiplier = jnp.zeros((SEQUENCE_TOKENS, MODEL_WIDTH), jnp.float32)
    for spike_index in range(4):
        log_multiplier = log_multiplier + jnp.where(token_positions >= spike_position[spike_index], spike_decrease[spike_index][None, :], 0.0)
    taps_out = rough_part * jnp.exp(log_multiplier - token_positions / decay_len) / jnp.sqrt(decay_len)
    taps_out = taps_out + jnp.where(token_positions == 0.0, direct, 0.0)
    return taps_out.astype(jnp.float32)


def strengthened(array, key, source, target, parts, factor):
    owner, partner = [(jnp.arange(array.shape[axis_at]) // (array.shape[axis_at] // parts)).reshape([-1 if axis == axis_at else 1 for axis in range(array.ndim)]) for axis_at in (source, target)]
    chosen = jax.random.permutation(key, parts)[partner]
    strong = (owner == chosen) | (owner == (partner + parts // 2) % parts)
    return jnp.where(strong, factor * array, array)


def steps_of(stream_key, extent, shards, low, top_value):
    def one(axis_at, blocks):
        heights = jax.random.uniform(jax.random.fold_in(jax.random.fold_in(stream_key, 6), axis_at), (blocks,), jnp.float32, low / len(shards), top_value / len(shards))
        return jnp.repeat(jnp.exp(heights), extent[axis_at] // blocks).reshape((-1,) + (1,) * (len(extent) - axis_at - 1))

    gain = one(*shards[0])
    for cut in shards[1:]:
        gain = gain * one(*cut)
    return gain


def centred(key, shape, spread, limit, cuts=(), held_as=jnp.bfloat16):
    array = spread * jax.random.normal(key, shape, jnp.float32)
    if cuts:
        array = array * steps_of(key, shape, cuts, -0.22, 0.18)
    return jnp.clip(array, -limit, limit).astype(held_as)


def heavy_noise(own_key, dims, width, reach, cuts, heavy, kind=jnp.bfloat16):
    array = width * jax.random.normal(own_key, dims, jnp.float32)
    if cuts:
        array = array * steps_of(own_key, dims, cuts, -0.22, 0.18)
    return jnp.clip(strengthened(array, jax.random.fold_in(own_key, 3), *heavy), -reach, reach).astype(kind)


def setup_inputs(seed: int = 0) -> dict:
    splits = jax.random.split(jax.random.key(seed), 5)
    return {
        "proj": centred(splits[0], (SEQUENCE_TOKENS, 3, MODEL_WIDTH), 1.0, 6.0, ((0, 32), (2, 8))),
        "short_filter": centred(splits[1], (3, TAPS, MODEL_WIDTH), 0.6, 3.0, ((2, 8),), jnp.float32),
        "long_filter": draw_long_filter(jax.random.fold_in(splits[4], 71), 0),
        "out_weight": heavy_noise(splits[3], (MODEL_WIDTH, MODEL_WIDTH), MODEL_WIDTH ** -0.5, 0.125, ((0, 8),), (0, 1, 8, 2.0)),
    }


def short_filtering(proj_block, short_block):
    values = proj_block.astype(jnp.float32)
    length_rows = values.shape[0]
    result = jnp.zeros(values.shape, jnp.float32)
    for tap_index in range(TAPS):
        shifted = jnp.pad(values, ((tap_index, 0), (0, 0), (0, 0)))[:length_rows]
        result = result + short_block[:, tap_index, :][None] * shifted
    return result


def causal_conv(signal, long_block):
    length_rows = signal.shape[0]
    padded_len = 2 * length_rows
    signal_hat = jnp.fft.rfft(signal, n=padded_len, axis=0)
    taps_hat = jnp.fft.rfft(long_block, n=padded_len, axis=0)
    return jnp.fft.irfft(signal_hat * taps_hat, n=padded_len, axis=0)[:length_rows]


def reference(proj, short_filter, long_filter, out_weight):
    block_width = math.gcd(MODEL_WIDTH, 256)
    block_count = MODEL_WIDTH // block_width

    def per_block(block_index):
        offset = block_index * block_width
        proj_block = lax.dynamic_slice_in_dim(proj, offset, block_width, 2)
        short_block = lax.dynamic_slice_in_dim(short_filter, offset, block_width, 2)
        long_block = lax.dynamic_slice_in_dim(long_filter, offset, block_width, 1)
        featured = short_filtering(proj_block, short_block)
        gated_in = (featured[:, 1, :] * featured[:, 2, :]).astype(jnp.bfloat16)
        convolved = causal_conv(gated_in.astype(jnp.float32), long_block).astype(jnp.bfloat16)
        return (featured[:, 0, :] * convolved.astype(jnp.float32)).astype(jnp.bfloat16)

    gathered = lax.map(per_block, jnp.arange(block_count, dtype=jnp.int32))
    gated_out = jnp.transpose(gathered, (1, 0, 2)).reshape(SEQUENCE_TOKENS, MODEL_WIDTH)
    row_block = math.gcd(SEQUENCE_TOKENS, 4096)

    def project(block_index):
        offset = block_index * row_block
        rows_part = lax.dynamic_slice_in_dim(gated_out, offset, row_block, 0)
        return jnp.dot(rows_part, out_weight, preferred_element_type=jnp.float32).astype(jnp.bfloat16)

    projected = lax.map(project, jnp.arange(SEQUENCE_TOKENS // row_block, dtype=jnp.int32))
    return projected.reshape(SEQUENCE_TOKENS, MODEL_WIDTH)
```

```python
import functools

import jax
import jax.numpy as jnp
import numpy as np
from jax import lax
from jax.experimental import pallas as pl
from jax.experimental.pallas import tpu as pltpu
from jax.sharding import Mesh, PartitionSpec as P

CTX = ("z", "yl", "core")
SIDE = 128
LENGTH = SIDE * SIDE
f32, bf16 = jnp.float32, jnp.bfloat16


def halves(table):
    high = table.astype(bf16)
    low = (table - high.astype(np.float64)).astype(bf16)
    return np.stack([high, low])


def tables():
    i = np.arange(SIDE)
    first = 2 * np.pi * np.outer(i + 0.25, i) / SIDE
    turn = 2 * np.pi * np.outer(i + 0.25, i) / LENGTH
    second = 2 * np.pi * np.outer(i, i) / SIDE
    c1, s1, c2, s2 = np.cos(first), np.sin(first), np.cos(second), np.sin(second)
    fwd1 = np.concatenate([c1, s1], 0)
    fwd2 = np.block([[c2, s2], [-s2, c2]])
    inv1 = np.block([[c2, -s2], [s2, c2]])
    inv2 = np.concatenate([c1.T, s1.T], 1) / LENGTH
    twist = np.stack([np.cos(turn), np.sin(turn)]).astype(np.float32)
    return halves(fwd1), halves(fwd2), halves(inv1), halves(inv2), twist


def split(x):
    high = x.astype(bf16)
    return high, (x - high.astype(f32)).astype(bf16)


def mm(a, b):
    return jnp.dot(a, b, preferred_element_type=f32)


def left3(tab, x):
    high, low = split(x)
    return mm(tab[0], high) + (mm(tab[1], high) + mm(tab[0], low))


def right3(x, tab):
    high, low = split(x)
    return mm(high, tab[0]) + (mm(low, tab[0]) + mm(high, tab[1]))


def forward(first, twist, tab2):
    spectra = []
    tc, ts = twist[0], twist[1]
    for w in range(first.shape[1] // SIDE):
        re, im = first[:SIDE, w * SIDE : (w + 1) * SIDE], first[SIDE:, w * SIDE : (w + 1) * SIDE]
        turned = jnp.concatenate([re * tc - im * ts, re * ts + im * tc], 1)
        spectra.append(right3(turned, tab2))
    return spectra


def filter_kernel(h_ref, fwd1_ref, fwd2_ref, twist_ref, out_ref, rows):
    channels = h_ref.shape[0]
    for n in range(SIDE):
        rows[n * channels : (n + 1) * channels, :] = h_ref[:, n * SIDE : (n + 1) * SIDE]

    def step(p, carry):
        pair = [rows[pl.ds(2 * p + w, SIDE, stride=channels), :] for w in range(2)]
        first = left3(fwd1_ref, jnp.concatenate(pair, 1))
        for w, spectrum in enumerate(forward(first, twist_ref, fwd2_ref)):
            out_ref[2 * p + w] = spectrum
        return carry

    lax.fori_loop(0, channels // 2, step, 0)


def conv_kernel(u_ref, h_ref, fwd1_ref, fwd2_ref, inv1_ref, inv2_ref, twist_ref, out_ref, rows, back):
    blocks, channels, local = u_ref.shape
    per = local // SIDE
    for i in range(blocks):
        for q in range(per):
            n = i * per + q
            rows[n * channels : (n + 1) * channels, :] = u_ref[i, :, q * SIDE : (q + 1) * SIDE].astype(f32)

    def step(p, carry):
        pair = jnp.concatenate([rows[pl.ds(2 * p + w, SIDE, stride=channels), :] for w in range(2)], 1).astype(bf16)
        first = mm(fwd1_ref[0], pair) + mm(fwd1_ref[1], pair)
        tc, ts = twist_ref[0], twist_ref[1]
        turned = []
        for w, s in enumerate(forward(first, twist_ref, fwd2_ref)):
            h = h_ref[2 * p + w]
            sr, si, hr, hi = s[:, :SIDE], s[:, SIDE:], h[:, :SIDE], h[:, SIDE:]
            product = jnp.concatenate([sr * hr - si * hi, sr * hi + si * hr], 1)
            b = right3(product, inv1_ref)
            br, bi = b[:, :SIDE], b[:, SIDE:]
            turned.append(jnp.concatenate([br * tc + bi * ts, bi * tc - br * ts], 0))
        y = left3(inv2_ref, jnp.concatenate(turned, 1))
        for w in range(2):
            back[pl.ds(2 * p + w, SIDE, stride=channels), :] = y[:, w * SIDE : (w + 1) * SIDE]
        return carry

    lax.fori_loop(0, channels // 2, step, 0)
    for i in range(blocks):
        for q in range(per):
            n = i * per + q
            out_ref[i, :, q * SIDE : (q + 1) * SIDE] = back[n * channels : (n + 1) * channels, :].astype(bf16)


def featured(x_ref, edge_ref, taps_ref, ext, s):
    tokens = x_ref.shape[1]
    count = taps_ref.shape[1]
    ext[8 : 8 + tokens, :] = x_ref[s].astype(f32)
    ext[8 - (count - 1) : 8, :] = edge_ref[s].astype(f32)
    total = taps_ref[s, 0:1, :] * ext[8 : 8 + tokens, :]
    for j in range(1, count):
        total = total + taps_ref[s, j : j + 1, :] * ext[8 - j : 8 - j + tokens, :]
    return total


def gate_in_kernel(x_ref, edge_ref, taps_ref, out_ref, ext):
    product = featured(x_ref, edge_ref, taps_ref, ext, 1) * featured(x_ref, edge_ref, taps_ref, ext, 2)
    out_ref[...] = product.T.astype(bf16)


def gate_out_kernel(x_ref, edge_ref, taps_ref, conv_ref, out_ref, ext):
    conv = conv_ref[...].astype(f32).T
    out_ref[...] = (featured(x_ref, edge_ref, taps_ref, ext, 0) * conv).astype(bf16)


def ring(axis, shift):
    size = lax.axis_size(axis)
    return [(i, (i + shift) % size) for i in range(size)]


def call(kernel, shape, dtype, scratch, flops, *args):
    moved = sum(a.size * a.dtype.itemsize for a in args)
    return pl.pallas_call(
        kernel,
        out_shape=jax.ShapeDtypeStruct(shape, dtype),
        scratch_shapes=scratch,
        cost_estimate=pl.CostEstimate(flops=flops, bytes_accessed=moved, transcendentals=0),
    )(*args)


def body(proj, short_filter, long_filter, out_weight):
    tokens, streams, width = proj.shape
    count = short_filter.shape[1]
    ctx = lax.axis_size(CTX)
    mine = width // ctx
    fwd1, fwd2, inv1, inv2, twist = [jnp.asarray(t) for t in tables()]

    streams_first = jnp.transpose(proj, (1, 0, 2))
    edge = lax.ppermute(
        streams_first[:, tokens - (count - 1) :, :], CTX, [(i, i + 1) for i in range(ctx - 1)]
    )

    nx, ny = lax.axis_size("x"), lax.axis_size("yh")
    x, yh = lax.axis_index("x"), lax.axis_index("yh")
    cols = out_weight.shape[1] // (nx * ny)

    def columns(shift, other):
        to = (x + shift) % nx
        row = (yh + other) % ny
        return lax.dynamic_slice_in_dim(out_weight, (row * nx + to) * cols, cols, 1)

    shifts = (2, 1, 3)
    weight_own, weight_other = {0: columns(0, 0)}, {0: columns(0, 1)}
    for s in shifts:
        both = jnp.concatenate([columns(s, 0), columns(s, 1)], 0)
        got = lax.ppermute(both, "x", ring("x", s))
        weight_own[s], weight_other[s] = got[:width], got[width:]

    ext = [pltpu.VMEM((tokens + 8, width), f32)]
    gated_in = call(gate_in_kernel, (width, tokens), bf16, ext, 0, streams_first, edge, short_filter)
    signal = lax.all_to_all(gated_in.reshape(ctx, mine, tokens), CTX, 0, 0)
    rows = [pltpu.VMEM((SIDE * mine, SIDE), f32)]
    spectrum = call(
        filter_kernel, (mine, SIDE, 2 * SIDE), f32, rows, 10**9, long_filter.T, fwd1, fwd2, twist
    )
    convolved = call(
        conv_kernel, (ctx, mine, tokens), bf16, rows * 2, 3 * 10**9,
        signal, spectrum, fwd1, fwd2, inv1, inv2, twist,
    )
    returned = lax.all_to_all(convolved, CTX, 0, 0).reshape(width, tokens)
    gated_out = call(
        gate_out_kernel, (tokens, width), bf16, ext, 0, streams_first, edge, short_filter, returned
    )
    pieces = {0: gated_out}
    for s in shifts:
        pieces[s] = lax.ppermute(gated_out, "x", ring("x", s))

    def project(weights):
        total = mm(pieces[0], weights[0])
        for s in (1, 3, 2):
            total = total + mm(pieces[s], weights[s])
        return total

    theirs = lax.ppermute(project(weight_other).astype(bf16), "yh", ring("yh", 1))
    return (project(weight_own) + theirs.astype(f32)).astype(bf16)


def solution(mesh):
    axes = Mesh(mesh.devices.reshape(8, 2, 2, 2, 4), ("z", "yl", "core", "yh", "x"))
    tp = ("yh", "x")
    placed = (P(CTX, None, tp), P(None, None, tp), P(None, tp + CTX), P(tp, None))
    return jax.shard_map(body, mesh=axes, in_specs=placed, out_specs=P(CTX, tp), check_vma=False)
```

```python
import jax
import jax.numpy as jnp
import numpy as np
from jax import lax
from jax.experimental import pallas as pl
from jax.experimental.pallas import tpu as pltpu
from jax.sharding import Mesh, PartitionSpec as P


CTX = ("z", "yl", "core")
SIDE = 128
LENGTH = SIDE * SIDE
WIDE = 4
EDGE = 8
LIMIT = 16 * 2**20
FULL = 60 * 1024 * 2**10
f32, bf16 = jnp.float32, jnp.bfloat16


def halves(table):
    high = table.astype(bf16)
    low = (table - high.astype(np.float64)).astype(bf16)
    return np.stack([high, low])


def tables():
    i = np.arange(SIDE)
    first = 2 * np.pi * np.outer(i + 0.25, i) / SIDE
    turn = 2 * np.pi * np.outer(i + 0.25, i) / LENGTH
    second = 2 * np.pi * np.outer(i, i) / SIDE
    c1, s1, c2, s2 = np.cos(first), np.sin(first), np.cos(second), np.sin(second)
    fwd1 = np.concatenate([c1, s1], 0)
    fwd2 = np.block([[c2, s2], [-s2, c2]])
    inv1 = np.block([[c2, -s2], [s2, c2]])
    inv2 = np.concatenate([c1.T, s1.T], 1) / LENGTH
    twist = np.stack([np.cos(turn), np.sin(turn)]).astype(np.float32)
    return halves(fwd1), halves(fwd2), halves(inv1), halves(inv2), twist


def split(x):
    high = x.astype(bf16)
    return high, (x - high.astype(f32)).astype(bf16)


def mm(a, b):
    return jnp.dot(a, b, preferred_element_type=f32)


def left3(tab, x):
    high, low = split(x)
    return mm(tab[0], high) + (mm(tab[1], high) + mm(tab[0], low))


def right3(x, tab):
    high, low = split(x)
    return mm(high, tab[0]) + (mm(low, tab[0]) + mm(high, tab[1]))


def stacked(first, twist):
    tc, ts = twist[0], twist[1]
    turned = []
    for w in range(first.shape[1] // SIDE):
        re, im = first[:SIDE, w * SIDE : (w + 1) * SIDE], first[SIDE:, w * SIDE : (w + 1) * SIDE]
        turned.append(jnp.concatenate([re * tc - im * ts, re * ts + im * tc], 1))
    return jnp.concatenate(turned, 0)


def filter_kernel(h_ref, fwd1_ref, fwd2_ref, twist_ref, out_ref, rows):
    channels = h_ref.shape[0]
    for n in range(SIDE):
        rows[n * channels : (n + 1) * channels, :] = h_ref[:, n * SIDE : (n + 1) * SIDE]

    def step(p, carry):
        group = [rows[pl.ds(WIDE * p + w, SIDE, stride=channels), :] for w in range(WIDE)]
        first = left3(fwd1_ref, jnp.concatenate(group, 1))
        spectra = right3(stacked(first, twist_ref), fwd2_ref)
        for w in range(WIDE):
            out_ref[WIDE * p + w] = spectra[w * SIDE : (w + 1) * SIDE]
        return carry

    lax.fori_loop(0, channels // WIDE, step, 0)


def fetch(sources, targets, sem):
    copies = [pltpu.make_async_copy(a, b, sem.at[i]) for i, (a, b) in enumerate(zip(sources, targets))]
    for c in copies:
        c.start()
    return copies


def conv_kernel(u_ref, *refs):
    sources, out_ref, rows, back, held, sem = refs[:6], refs[6], refs[7], refs[8], refs[9:15], refs[15]
    h_ref, fwd1_ref, fwd2_ref, inv1_ref, inv2_ref, twist_ref = held
    copies = fetch(sources, held, sem)
    blocks, channels, local = u_ref.shape
    per = local // SIDE
    for i in range(blocks):
        for q in range(per):
            n = i * per + q
            rows[n * channels : (n + 1) * channels, :] = u_ref[i, :, q * SIDE : (q + 1) * SIDE].astype(f32)
    for c in copies:
        c.wait()

    def step(p, carry):
        group = [rows[pl.ds(WIDE * p + w, SIDE, stride=channels), :] for w in range(WIDE)]
        group = jnp.concatenate(group, 1).astype(bf16)
        first = mm(fwd1_ref[0], group) + mm(fwd1_ref[1], group)
        spectra = right3(stacked(first, twist_ref), fwd2_ref)
        products = []
        for w in range(WIDE):
            s, h = spectra[w * SIDE : (w + 1) * SIDE], h_ref[WIDE * p + w]
            sr, si, hr, hi = s[:, :SIDE], s[:, SIDE:], h[:, :SIDE], h[:, SIDE:]
            products.append(jnp.concatenate([sr * hr - si * hi, sr * hi + si * hr], 1))
        b = right3(jnp.concatenate(products, 0), inv1_ref)
        tc, ts = twist_ref[0], twist_ref[1]
        turned = []
        for w in range(WIDE):
            br, bi = b[w * SIDE : (w + 1) * SIDE, :SIDE], b[w * SIDE : (w + 1) * SIDE, SIDE:]
            turned.append(jnp.concatenate([br * tc + bi * ts, bi * tc - br * ts], 0))
        y = left3(inv2_ref, jnp.concatenate(turned, 1))
        for w in range(WIDE):
            back[pl.ds(WIDE * p + w, SIDE, stride=channels), :] = y[:, w * SIDE : (w + 1) * SIDE]
        return carry

    lax.fori_loop(0, channels // WIDE, step, 0)
    for i in range(blocks):
        for q in range(per):
            n = i * per + q
            out_ref[i, :, q * SIDE : (q + 1) * SIDE] = back[n * channels : (n + 1) * channels, :].astype(bf16)


def featured(x, edge_ref, taps_ref, ext, s):
    tokens = x.shape[0]
    ext[EDGE : EDGE + tokens, :] = x.astype(f32)
    ext[:EDGE, :] = edge_ref[s].astype(f32)
    total = taps_ref[s, 0:1, :] * ext[EDGE : EDGE + tokens, :]
    for j in range(1, taps_ref.shape[1]):
        total = total + taps_ref[s, j : j + 1, :] * ext[EDGE - j : EDGE - j + tokens, :]
    return total


def gate_in_kernel(edge_ref, x_hbm, taps_hbm, out_ref, ext, keys, values, taps, sem):
    copies = fetch((taps_hbm, x_hbm.at[1], x_hbm.at[2]), (taps, keys, values), sem)
    copies[0].wait()
    copies[1].wait()
    key = featured(keys[...], edge_ref, taps, ext, 1)
    copies[2].wait()
    out_ref[...] = (key * featured(values[...], edge_ref, taps, ext, 2)).T.astype(bf16)


def query_kernel(x_ref, edge_ref, taps_ref, out_ref, ext):
    out_ref[...] = featured(x_ref[0], edge_ref, taps_ref, ext, 0)


def gate_out_kernel(query_ref, conv_ref, upper_ref, lower_ref):
    gated = (query_ref[...] * conv_ref[...].astype(f32).T).astype(bf16)
    half = upper_ref.shape[0]
    upper_ref[...] = gated[:half]
    lower_ref[...] = gated[half:]


def block_columns(nx, ny, shift, other, cols):
    x, yh = lax.axis_index("x"), lax.axis_index("yh")
    block = ((yh + other) % ny) * nx + (x + shift) % nx
    return pl.ds(pl.multiple_of(block * cols, cols), cols)


def columns_kernel(nx, ny, weight_ref, *rest):
    outs, sem = rest[:nx], rest[nx]
    cols = outs[0].shape[2]
    half = weight_ref.shape[0] // 2
    first = pl.multiple_of(lax.axis_index("core") * half, half)
    sources = []
    for s in range(nx):
        for o in range(ny):
            at = block_columns(nx, ny, s, o, cols)
            sources.append(weight_ref.at[pl.ds(first, half), at] if s else weight_ref.at[:, at])
    for c in fetch(sources, [out.at[o] for out in outs for o in range(ny)], sem):
        c.wait()


def stage_kernel(*refs):
    count = len(refs) // 2
    for c in fetch(refs[:count], refs[count : 2 * count], refs[2 * count]):
        c.wait()


def project_rows(other, at, pieces, weights):
    width = pieces[0].shape[1]
    half = width // 2
    core = lax.axis_index("core")
    mine = pl.ds(pl.multiple_of(core * half, half), half)
    rest = pl.ds(pl.multiple_of((1 - core) * half, half), half)
    total = mm(pieces[0][at, :], weights[0][other])
    for s, piece in enumerate(pieces[1:]):
        total = total + mm(piece[at, mine], weights[1 + 2 * s][other])
        total = total + mm(piece[at, rest], weights[2 + 2 * s][other])
    return total


def project_other_kernel(*refs):
    pieces, weights, out_ref = refs[:4], refs[4:11], refs[11]
    step = 128

    def rows(r, carry):
        at = pl.ds(pl.multiple_of(r * step, step), step)
        out_ref[at, :] = project_rows(1, at, pieces, weights).astype(out_ref.dtype)
        return carry

    lax.fori_loop(0, out_ref.shape[0] // step, rows, 0)


def project_own_kernel(*refs):
    pieces, weights, out_ref = refs[:8], refs[8:15], refs[15]
    step = 128
    tokens = pieces[0].shape[0]
    for part in range(2):

        def rows(r, carry):
            start = pl.multiple_of(r * step, step)
            sums = project_rows(0, pl.ds(start, step), pieces[4 * part : 4 * part + 4], weights)
            out_ref[pl.ds(part * tokens + start, step), :] = sums
            return carry

        lax.fori_loop(0, tokens // step, rows, 0)


def finish_kernel(own_ref, first_ref, second_ref, out_ref):
    tokens = first_ref.shape[0]
    for part, came in enumerate((first_ref, second_ref)):
        at = slice(part * tokens, (part + 1) * tokens)
        out_ref[at, :] = (own_ref[at, :] + came[...].astype(f32)).astype(out_ref.dtype)


def ring(axis, shift):
    size = lax.axis_size(axis)
    return [(i, (i + shift) % size) for i in range(size)]


VM = pl.BlockSpec(memory_space=pltpu.VMEM)
HBM = pl.BlockSpec(memory_space=pltpu.HBM)


def held(*arrays):
    return [pltpu.VMEM(a.shape, a.dtype) for a in arrays] + [pltpu.SemaphoreType.DMA((len(arrays),))]


def call(kernel, outs, scratch, flops, *args, specs=None, limit=LIMIT):
    moved = sum(a.size * a.dtype.itemsize for a in args)
    shapes = [jax.ShapeDtypeStruct(*o) for o in outs]
    result = pl.pallas_call(
        kernel,
        out_shape=shapes,
        in_specs=specs or [VM] * len(args),
        out_specs=[VM] * len(shapes),
        scratch_shapes=scratch,
        compiler_params=pltpu.CompilerParams(vmem_limit_bytes=limit),
        cost_estimate=pl.CostEstimate(flops=flops, bytes_accessed=moved, transcendentals=0),
    )(*args)
    return result if len(shapes) > 1 else result[0]


def body(proj, short_filter, long_filter, out_weight):
    tokens, _, width = proj.shape
    ctx = lax.axis_size(CTX)
    mine = width // ctx
    nx, ny = lax.axis_size("x"), lax.axis_size("yh")
    cols = out_weight.shape[1] // (nx * ny)
    fwd1, fwd2, inv1, inv2, twist = [jnp.asarray(t) for t in tables()]

    streams_first = jnp.transpose(proj, (1, 0, 2))
    edge = lax.ppermute(streams_first[:, tokens - EDGE :, :], CTX, [(i, i + 1) for i in range(ctx - 1)])
    ext = [pltpu.VMEM((tokens + EDGE, width), f32)]
    gated_in = call(
        gate_in_kernel, [((width, tokens), bf16)],
        ext + held(streams_first[1], streams_first[2], short_filter), 0,
        edge, streams_first, short_filter, specs=[VM, HBM, HBM], limit=FULL,
    )
    gated_in, out_weight = lax.optimization_barrier((gated_in, out_weight))
    signal = lax.all_to_all(gated_in.reshape(ctx, mine, tokens), CTX, 0, 0)

    def columns(*refs):
        columns_kernel(nx, ny, *refs)

    blocks = call(
        columns, [((ny, width if s == 0 else width // 2, cols), bf16) for s in range(nx)],
        [pltpu.SemaphoreType.DMA((ny * nx,))], 0, out_weight, specs=[HBM], limit=FULL,
    )
    weights = [blocks[0]]
    for s in range(1, nx):
        came = lax.ppermute(blocks[s], "x", ring("x", s))
        weights += [came, lax.ppermute(came, "core", ring("core", 1))]

    rows = [pltpu.VMEM((SIDE * mine, SIDE), f32)]
    spectrum = call(filter_kernel, [((mine, SIDE, 2 * SIDE), f32)], rows, 10**9, long_filter.T, fwd1, fwd2, twist)
    convolved = call(
        conv_kernel, [((ctx, mine, tokens), bf16)],
        rows * 2 + held(spectrum, fwd1, fwd2, inv1, inv2, twist), 3 * 10**9,
        signal, spectrum, fwd1, fwd2, inv1, inv2, twist, specs=[VM] + [HBM] * 6, limit=FULL,
    )
    returned = lax.all_to_all(convolved, CTX, 0, 0).reshape(width, tokens)
    query = call(query_kernel, [((tokens, width), f32)], ext, 0, streams_first, edge, short_filter)
    half = tokens // 2
    upper, lower = call(gate_out_kernel, [((half, width), bf16)] * 2, [], 0, query, returned)

    def send(block, shift):
        return lax.ppermute(block, "x", ring("x", shift))

    left_upper, right_lower = send(upper, 1), send(lower, -1)
    right_upper, left_lower = send(upper, -1), send(lower, 1)
    far_upper, far_lower = send(left_upper, 1), send(right_lower, -1)
    pieces = [(upper, left_upper, far_upper, right_upper), (lower, left_lower, far_lower, right_lower)]

    weights = call(
        stage_kernel, [(w.shape, bf16) for w in weights], [pltpu.SemaphoreType.DMA((len(weights),))], 0,
        *weights, specs=[HBM] * len(weights),
    )
    theirs = []
    for part in range(2):
        sums = call(project_other_kernel, [((half, cols), bf16)], [], 10**9, *pieces[part], *weights)
        theirs.append(lax.ppermute(sums, "yh", ring("yh", 1)))
    own = call(project_own_kernel, [((tokens, cols), f32)], [], 2 * 10**9, *pieces[0], *pieces[1], *weights)
    return call(finish_kernel, [((tokens, cols), bf16)], [], 0, own, *theirs)


def solution(mesh):
    axes = Mesh(mesh.devices.reshape(8, 2, 2, 2, 4), ("z", "yl", "core", "yh", "x"))
    tp = ("yh", "x")
    placed = (P(CTX, None, tp), P(None, None, tp), P(None, tp + CTX), P(tp, None))
    return jax.shard_map(body, mesh=axes, in_specs=placed, out_specs=P(CTX, tp), check_vma=False)
```

```python
import jax
import jax.numpy as jnp
import numpy as np
from jax import lax
from jax.experimental import pallas as pl
from jax.experimental.pallas import tpu as pltpu
from jax.sharding import Mesh, PartitionSpec as P


CTX = ("z", "yl", "core")
SIDE = 128
LENGTH = SIDE * SIDE
EDGE = 8
LIMIT = 16 * 2**20
f32, bf16 = jnp.float32, jnp.bfloat16


def halves(table):
    high = table.astype(bf16)
    low = (table - high.astype(np.float64)).astype(bf16)
    return np.stack([high, low])


def tables():
    i = np.arange(SIDE)
    first = 2 * np.pi * np.outer(i + 0.25, i) / SIDE
    turn = 2 * np.pi * np.outer(i + 0.25, i) / LENGTH
    second = 2 * np.pi * np.outer(i, i) / SIDE
    c1, s1, c2, s2 = np.cos(first), np.sin(first), np.cos(second), np.sin(second)
    fwd1 = np.concatenate([c1, s1], 0)
    fwd2 = np.block([[c2, s2], [-s2, c2]])
    inv2 = np.concatenate([c1.T, s1.T], 1) / LENGTH
    twist = np.stack([np.cos(turn), np.sin(turn)]).astype(np.float32)
    return halves(fwd1), halves(fwd2), halves(inv2), twist


def split(x):
    high = x.astype(bf16)
    return high, (x - high.astype(f32)).astype(bf16)


def mm(a, b):
    return jnp.dot(a, b, preferred_element_type=f32)


def left3(tab, x):
    high, low = split(x)
    return mm(tab[0], high) + (mm(tab[1], high) + mm(tab[0], low))


def right3(x, tab):
    high, low = split(x)
    return mm(high, tab[0]) + (mm(low, tab[0]) + mm(high, tab[1]))


def stacked(first, twist):
    tc, ts = twist[0], twist[1]
    turned = []
    for w in range(first.shape[1] // SIDE):
        re, im = first[:SIDE, w * SIDE : (w + 1) * SIDE], first[SIDE:, w * SIDE : (w + 1) * SIDE]
        turned.append(jnp.concatenate([re * tc - im * ts, re * ts + im * tc], 1))
    return jnp.concatenate(turned, 0)


def filter_kernel(h_ref, fwd1_ref, fwd2_ref, twist_ref, out_ref, rows):
    channels = h_ref.shape[0]
    for n in range(SIDE):
        rows[n * channels : (n + 1) * channels, :] = h_ref[:, n * SIDE : (n + 1) * SIDE]

    group = jnp.concatenate([rows[pl.ds(w, SIDE, stride=channels), :] for w in range(channels)], 1)
    spectra = right3(stacked(left3(fwd1_ref, group), twist_ref), fwd2_ref)
    for w in range(channels):
        out_ref[w] = spectra[w * SIDE : (w + 1) * SIDE]


def fetch(sources, targets, sem):
    copies = [pltpu.make_async_copy(a, b, sem.at[i]) for i, (a, b) in enumerate(zip(sources, targets))]
    for c in copies:
        c.start()
    return copies


def conv_kernel(u_ref, *refs):
    sources, out_hbm, rows, back, out_ref = refs[:5], refs[5], refs[6], refs[7], refs[8]
    held, sem, out_sem = refs[9:14], refs[14], refs[15]
    fwd1_ref, twist_ref, fwd2_ref, h_ref, inv2_ref = held
    copies = fetch(sources, held, sem)
    blocks, channels, local = u_ref.shape
    per = local // SIDE
    for i in range(blocks):
        for q in range(per):
            n = i * per + q
            rows[n * channels : (n + 1) * channels, :] = u_ref[i, :, q * SIDE : (q + 1) * SIDE].astype(f32)
    group = jnp.concatenate([rows[pl.ds(w, SIDE, stride=channels), :] for w in range(channels)], 1).astype(bf16)
    for c in copies[:3]:
        c.wait()
    first = mm(fwd1_ref[0], group) + mm(fwd1_ref[1], group)
    spectra = right3(stacked(first, twist_ref), fwd2_ref)
    for c in copies[3:]:
        c.wait()
    products = []
    for w in range(channels):
        s, h = spectra[w * SIDE : (w + 1) * SIDE], h_ref[w]
        sr, si, hr, hi = s[:, :SIDE], s[:, SIDE:], h[:, :SIDE], h[:, SIDE:]
        products.append(jnp.concatenate([sr * hr - si * hi, -(sr * hi + si * hr)], 1))
    b = right3(jnp.concatenate(products, 0), fwd2_ref)
    tc, ts = twist_ref[0], twist_ref[1]
    turned = []
    for w in range(channels):
        br, bi = b[w * SIDE : (w + 1) * SIDE, :SIDE], b[w * SIDE : (w + 1) * SIDE, SIDE:]
        turned.append(jnp.concatenate([br * tc - bi * ts, -(bi * tc + br * ts)], 0))
    y = left3(inv2_ref, jnp.concatenate(turned, 1))
    for w in range(channels):
        back[pl.ds(w, SIDE, stride=channels), :] = y[:, w * SIDE : (w + 1) * SIDE]
    outs = []
    for i in range(blocks):
        for q in range(per):
            n = i * per + q
            out_ref[i, :, q * SIDE : (q + 1) * SIDE] = back[n * channels : (n + 1) * channels, :].astype(bf16)
        if (i + 1) % (blocks // 4) == 0:
            at = pl.ds(i + 1 - blocks // 4, blocks // 4)
            outs.append(pltpu.make_async_copy(out_ref.at[at], out_hbm.at[at], out_sem.at[len(outs)]))
            outs[-1].start()
    for c in outs:
        c.wait()


def featured(x, edge_ref, taps_ref, ext, s):
    tokens = x.shape[0]
    ext[EDGE : EDGE + tokens, :] = x.astype(f32)
    ext[:EDGE, :] = edge_ref[s].astype(f32)
    total = taps_ref[s, 0:1, :] * ext[EDGE : EDGE + tokens, :]
    for j in range(1, taps_ref.shape[1]):
        total = total + taps_ref[s, j : j + 1, :] * ext[EDGE - j : EDGE - j + tokens, :]
    return total


def gate_in_kernel(edge_ref, x_hbm, taps_hbm, out_ref, ext, keys, values, taps, sem):
    copies = fetch((taps_hbm, x_hbm.at[1], x_hbm.at[2]), (taps, keys, values), sem)
    copies[0].wait()
    copies[1].wait()
    key = featured(keys[...], edge_ref, taps, ext, 1)
    copies[2].wait()
    out_ref[...] = (key * featured(values[...], edge_ref, taps, ext, 2)).T.astype(bf16)


def query_kernel(x_ref, edge_ref, taps_ref, out_ref, ext):
    out_ref[...] = featured(x_ref[0], edge_ref, taps_ref, ext, 0)


def gate_out_kernel(query_ref, conv_ref, upper_ref, lower_ref):
    gated = (query_ref[...] * conv_ref[...].astype(f32).T).astype(bf16)
    half = upper_ref.shape[0]
    upper_ref[...] = gated[:half]
    lower_ref[...] = gated[half:]


def block_columns(nx, ny, shift, other, cols):
    x, yh = lax.axis_index("x"), lax.axis_index("yh")
    block = ((yh + other) % ny) * nx + (x + shift) % nx
    return pl.ds(pl.multiple_of(block * cols, cols), cols)


def columns_kernel(nx, ny, weight_ref, *rest):
    outs, sem = rest[:nx], rest[nx]
    cols = outs[0].shape[2]
    half = weight_ref.shape[0] // 2
    first = pl.multiple_of(lax.axis_index("core") * half, half)
    sources = []
    for s in range(nx):
        for o in range(ny):
            at = block_columns(nx, ny, s, o, cols)
            sources.append(weight_ref.at[pl.ds(first, half), at] if s else weight_ref.at[:, at])
    for c in fetch(sources, [out.at[o] for out in outs for o in range(ny)], sem):
        c.wait()


def stage_kernel(*refs):
    count = len(refs) // 2
    for c in fetch(refs[:count], refs[count : 2 * count], refs[2 * count]):
        c.wait()


def project_rows(other, at, pieces, weights):
    width = pieces[0].shape[1]
    half = width // 2
    core = lax.axis_index("core")
    mine = pl.ds(pl.multiple_of(core * half, half), half)
    rest = pl.ds(pl.multiple_of((1 - core) * half, half), half)
    total = mm(pieces[0][at, :], weights[0][other])
    for s, piece in enumerate(pieces[1:]):
        total = total + mm(piece[at, mine], weights[1 + 2 * s][other])
        total = total + mm(piece[at, rest], weights[2 + 2 * s][other])
    return total


def project_other_kernel(*refs):
    pieces, weights, out_ref = refs[:4], refs[4:11], refs[11]
    step = 128

    def rows(r, carry):
        at = pl.ds(pl.multiple_of(r * step, step), step)
        out_ref[at, :] = project_rows(1, at, pieces, weights).astype(out_ref.dtype)
        return carry

    lax.fori_loop(0, out_ref.shape[0] // step, rows, 0)


def project_own_kernel(*refs):
    pieces, weights, out_ref = refs[:8], refs[8:15], refs[15]
    step = 128
    tokens = pieces[0].shape[0]
    for part in range(2):

        def rows(r, carry):
            start = pl.multiple_of(r * step, step)
            sums = project_rows(0, pl.ds(start, step), pieces[4 * part : 4 * part + 4], weights)
            out_ref[pl.ds(part * tokens + start, step), :] = sums
            return carry

        lax.fori_loop(0, tokens // step, rows, 0)


def finish_kernel(own_ref, first_ref, second_ref, out_ref):
    tokens = first_ref.shape[0]
    for part, came in enumerate((first_ref, second_ref)):
        at = slice(part * tokens, (part + 1) * tokens)
        out_ref[at, :] = (own_ref[at, :] + came[...].astype(f32)).astype(out_ref.dtype)


def ring(axis, shift):
    size = lax.axis_size(axis)
    return [(i, (i + shift) % size) for i in range(size)]


VM = pl.BlockSpec(memory_space=pltpu.VMEM)
HBM = pl.BlockSpec(memory_space=pltpu.HBM)


def held(*arrays):
    return [pltpu.VMEM(a.shape, a.dtype) for a in arrays] + [pltpu.SemaphoreType.DMA((len(arrays),))]


def call(kernel, outs, scratch, flops, *args, specs=None, outs_at=VM):
    specs = specs or [VM] * len(args)
    args = [pltpu.with_memory_space_constraint(a, pltpu.HBM) if s is HBM else a for a, s in zip(args, specs)]
    moved = sum(a.size * a.dtype.itemsize for a in args)
    shapes = [jax.ShapeDtypeStruct(*o) for o in outs]
    result = pl.pallas_call(
        kernel,
        out_shape=shapes,
        in_specs=specs,
        out_specs=[outs_at] * len(shapes),
        scratch_shapes=scratch,
        compiler_params=pltpu.CompilerParams(vmem_limit_bytes=LIMIT),
        cost_estimate=pl.CostEstimate(flops=flops, bytes_accessed=moved, transcendentals=0),
    )(*args)
    return result if len(shapes) > 1 else result[0]


def transform(long_filter, fwd1, fwd2, twist):
    mine = long_filter.shape[1]
    rows = [pltpu.VMEM((SIDE * mine, SIDE), f32)]
    return call(filter_kernel, [((mine, SIDE, 2 * SIDE), f32)], rows, 10**9, long_filter.T, fwd1, fwd2, twist)


def convolve(signal, spectrum, fwd1, fwd2, inv2, twist):
    mine = signal.shape[1]
    rows = [pltpu.VMEM((SIDE * mine, SIDE), f32)] * 2
    inside = [pltpu.VMEM(signal.shape, bf16)]
    kept = held(fwd1, twist, fwd2, spectrum, inv2)[:-1]
    sems = [pltpu.SemaphoreType.DMA((5,)), pltpu.SemaphoreType.DMA((4,))]
    return call(
        conv_kernel, [(signal.shape, bf16)], rows + inside + kept + sems, 3 * 10**9,
        signal, fwd1, twist, fwd2, spectrum, inv2, specs=[VM] + [HBM] * 5, outs_at=HBM,
    )


def body(proj, short_filter, long_filter, out_weight):
    tokens, _, width = proj.shape
    ctx = lax.axis_size(CTX)
    mine = width // ctx
    nx, ny = lax.axis_size("x"), lax.axis_size("yh")
    cols = out_weight.shape[1] // (nx * ny)
    fwd1, fwd2, inv2, twist = [jnp.asarray(t) for t in tables()]

    streams_first = jnp.transpose(proj, (1, 0, 2))
    edge = lax.ppermute(streams_first[:, tokens - EDGE :, :], CTX, [(i, i + 1) for i in range(ctx - 1)])
    ext = [pltpu.VMEM((tokens + EDGE, width), f32)]
    gated_in = call(
        gate_in_kernel, [((width, tokens), bf16)],
        ext + held(streams_first[1], streams_first[2], short_filter), 0,
        edge, streams_first, short_filter, specs=[VM, HBM, HBM],
    )
    gated_in, out_weight = lax.optimization_barrier((gated_in, out_weight))
    signal = lax.all_to_all(gated_in.reshape(ctx, mine, tokens), CTX, 0, 0)

    def columns(*refs):
        columns_kernel(nx, ny, *refs)

    blocks = call(
        columns, [((ny, width if s == 0 else width // 2, cols), bf16) for s in range(nx)],
        [pltpu.SemaphoreType.DMA((ny * nx,))], 0, out_weight, specs=[HBM],
    )
    weights = [blocks[0]]
    for s in range(1, nx):
        came = lax.ppermute(blocks[s], "x", ring("x", s))
        weights += [came, lax.ppermute(came, "core", ring("core", 1))]

    spectrum = transform(long_filter, fwd1, fwd2, twist)
    convolved = convolve(signal, spectrum, fwd1, fwd2, inv2, twist)
    returned = lax.all_to_all(convolved, CTX, 0, 0).reshape(width, tokens)
    query = call(query_kernel, [((tokens, width), f32)], ext, 0, streams_first, edge, short_filter)
    half = tokens // 2
    upper, lower = call(gate_out_kernel, [((half, width), bf16)] * 2, [], 0, query, returned)

    def send(block, shift):
        return lax.ppermute(block, "x", ring("x", shift))

    left_upper, right_lower = send(upper, 1), send(lower, -1)
    right_upper, left_lower = send(upper, -1), send(lower, 1)
    far_upper, far_lower = send(left_upper, 1), send(right_lower, -1)
    pieces = [(upper, left_upper, far_upper, right_upper), (lower, left_lower, far_lower, right_lower)]

    weights = call(
        stage_kernel, [(w.shape, bf16) for w in weights], [pltpu.SemaphoreType.DMA((len(weights),))], 0,
        *weights, specs=[HBM] * len(weights),
    )
    theirs = []
    for part in range(2):
        sums = call(project_other_kernel, [((half, cols), bf16)], [], 10**9, *pieces[part], *weights)
        theirs.append(lax.ppermute(sums, "yh", ring("yh", 1)))
    own = call(project_own_kernel, [((tokens, cols), f32)], [], 2 * 10**9, *pieces[0], *pieces[1], *weights)
    return call(finish_kernel, [((tokens, cols), bf16)], [], 0, own, *theirs)


def solution(mesh):
    axes = Mesh(mesh.devices.reshape(8, 2, 2, 2, 4), ("z", "yl", "core", "yh", "x"))
    tp = ("yh", "x")
    placed = (P(CTX, None, tp), P(None, None, tp), P(None, tp + CTX), P(tp, None))
    return jax.shard_map(body, mesh=axes, in_specs=placed, out_specs=P(CTX, tp), check_vma=False)
```

```python
import jax
import jax.numpy as jnp
import numpy as np
from jax import lax
from jax.experimental import pallas as pl
from jax.experimental.pallas import tpu as pltpu
from jax.sharding import Mesh, PartitionSpec as P


CTX = ("z", "yl", "core")
SIDE = 128
LENGTH = SIDE * SIDE
EDGE = 8
LIMIT = 16 * 2**20
f32, bf16 = jnp.float32, jnp.bfloat16


def halves(table):
    high = table.astype(bf16)
    low = (table - high.astype(np.float64)).astype(bf16)
    return np.stack([high, low])


def tables():
    i = np.arange(SIDE)
    first = 2 * np.pi * np.outer(i + 0.25, i) / SIDE
    turn = 2 * np.pi * np.outer(i + 0.25, i) / LENGTH
    second = 2 * np.pi * np.outer(i, i) / SIDE
    c1, s1, c2, s2 = np.cos(first), np.sin(first), np.cos(second), np.sin(second)
    fwd1 = np.concatenate([c1, s1], 0)
    fwd2 = np.block([[c2, s2], [-s2, c2]])
    inv2 = np.concatenate([c1.T, s1.T], 1) / LENGTH
    twist = np.stack([np.cos(turn), np.sin(turn)]).astype(np.float32)
    return np.concatenate(halves(fwd1), 1), halves(fwd2), halves(inv2), twist


def split(x):
    high = x.astype(bf16)
    return high, (x - high.astype(f32)).astype(bf16)


def mm(a, b):
    return jnp.dot(a, b, preferred_element_type=f32)


def left3(tab, x):
    high, low = split(x)
    return mm(tab[0], high) + (mm(tab[1], high) + mm(tab[0], low))


def right3(x, tab):
    high, low = split(x)
    return mm(high, tab[0]) + (mm(low, tab[0]) + mm(high, tab[1]))


def stacked(first, twist):
    tc, ts = twist[0], twist[1]
    turned = []
    for w in range(first.shape[1] // SIDE):
        re, im = first[:SIDE, w * SIDE : (w + 1) * SIDE], first[SIDE:, w * SIDE : (w + 1) * SIDE]
        turned.append(jnp.concatenate([re * tc - im * ts, re * ts + im * tc], 1))
    return jnp.concatenate(turned, 0)


def filter_kernel(h_ref, fwd1_ref, fwd2_ref, twist_ref, out_ref, rows):
    channels = h_ref.shape[0]
    for n in range(SIDE):
        rows[n * channels : (n + 1) * channels, :] = h_ref[:, n * SIDE : (n + 1) * SIDE]

    group = jnp.concatenate([rows[pl.ds(w, SIDE, stride=channels), :] for w in range(channels)], 1)
    high, low = split(group)
    first = mm(fwd1_ref[...], jnp.concatenate([high, high], 0)) + mm(fwd1_ref[:, :SIDE], low)
    spectra = right3(stacked(first, twist_ref), fwd2_ref)
    for w in range(channels):
        out_ref[w] = spectra[w * SIDE : (w + 1) * SIDE]


def fetch(sources, targets, sem):
    copies = [pltpu.make_async_copy(a, b, sem.at[i]) for i, (a, b) in enumerate(zip(sources, targets))]
    for c in copies:
        c.start()
    return copies


def conv_kernel(u_ref, *refs):
    sources, out_hbm, rows, back, out_ref = refs[:5], refs[5], refs[6], refs[7], refs[8]
    held, sem, out_sem = refs[9:14], refs[14], refs[15]
    fwd1_ref, twist_ref, fwd2_ref, h_ref, inv2_ref = held
    copies = fetch(sources, held, sem)
    blocks, channels, local = u_ref.shape
    per = local // SIDE
    for i in range(blocks):
        for q in range(per):
            n = i * per + q
            rows[n * channels : (n + 1) * channels, :] = u_ref[i, :, q * SIDE : (q + 1) * SIDE].astype(f32)
    group = jnp.concatenate([rows[pl.ds(w, SIDE, stride=channels), :] for w in range(channels)], 1).astype(bf16)
    for c in copies[:3]:
        c.wait()
    first = mm(fwd1_ref[...], jnp.concatenate([group, group], 0))
    spectra = right3(stacked(first, twist_ref), fwd2_ref)
    for c in copies[3:]:
        c.wait()
    products = []
    for w in range(channels):
        s, h = spectra[w * SIDE : (w + 1) * SIDE], h_ref[w]
        sr, si, hr, hi = s[:, :SIDE], s[:, SIDE:], h[:, :SIDE], h[:, SIDE:]
        products.append(jnp.concatenate([sr * hr - si * hi, -(sr * hi + si * hr)], 1))
    b = right3(jnp.concatenate(products, 0), fwd2_ref)
    tc, ts = twist_ref[0], twist_ref[1]
    turned = []
    for w in range(channels):
        br, bi = b[w * SIDE : (w + 1) * SIDE, :SIDE], b[w * SIDE : (w + 1) * SIDE, SIDE:]
        turned.append(jnp.concatenate([br * tc - bi * ts, -(bi * tc + br * ts)], 0))
    y = left3(inv2_ref, jnp.concatenate(turned, 1))
    for w in range(channels):
        back[pl.ds(w, SIDE, stride=channels), :] = y[:, w * SIDE : (w + 1) * SIDE]
    outs = []
    for i in range(blocks):
        for q in range(per):
            n = i * per + q
            out_ref[i, :, q * SIDE : (q + 1) * SIDE] = back[n * channels : (n + 1) * channels, :].astype(bf16)
        if (i + 1) % (blocks // 4) == 0:
            at = pl.ds(i + 1 - blocks // 4, blocks // 4)
            outs.append(pltpu.make_async_copy(out_ref.at[at], out_hbm.at[at], out_sem.at[len(outs)]))
            outs[-1].start()
    for c in outs:
        c.wait()


def featured(x, edge_ref, taps_ref, ext, s, cut=slice(None)):
    tokens = x.shape[0]
    ext[EDGE : EDGE + tokens, cut] = x.astype(f32)
    ext[:EDGE, cut] = edge_ref[s, :, cut].astype(f32)
    total = taps_ref[s, 0:1, cut] * ext[EDGE : EDGE + tokens, cut]
    for j in range(1, taps_ref.shape[1]):
        total = total + taps_ref[s, j : j + 1, cut] * ext[EDGE - j : EDGE - j + tokens, cut]
    return total


def gate_in_kernel(edge_ref, x_hbm, taps_hbm, out_hbm, ext, keys, values, taps, out_ref, sem, out_sem):
    parts = 4
    size = keys.shape[1] // parts
    cuts = [slice(p * size, (p + 1) * size) for p in range(parts)]
    sources, targets = [taps_hbm], [taps]
    for cut in cuts:
        sources += [x_hbm.at[1, :, cut], x_hbm.at[2, :, cut]]
        targets += [keys.at[:, cut], values.at[:, cut]]
    copies = fetch(sources, targets, sem)
    copies[0].wait()
    outs = []
    for p, cut in enumerate(cuts):
        copies[1 + 2 * p].wait()
        copies[2 + 2 * p].wait()
        key = featured(keys[:, cut], edge_ref, taps, ext, 1, cut)
        product = key * featured(values[:, cut], edge_ref, taps, ext, 2, cut)
        out_ref[cut, :] = product.T.astype(bf16)
        outs.append(pltpu.make_async_copy(out_ref.at[cut], out_hbm.at[cut], out_sem.at[p]))
        outs[-1].start()
    for c in outs:
        c.wait()


def query_kernel(x_ref, edge_ref, taps_ref, out_ref, ext):
    out_ref[...] = featured(x_ref[0], edge_ref, taps_ref, ext, 0)


def gate_out_kernel(query_ref, conv_ref, upper_ref, lower_ref):
    gated = (query_ref[...] * conv_ref[...].astype(f32).T).astype(bf16)
    half = upper_ref.shape[0]
    upper_ref[...] = gated[:half]
    lower_ref[...] = gated[half:]


def block_columns(nx, ny, shift, other, cols):
    x, yh = lax.axis_index("x"), lax.axis_index("yh")
    block = ((yh + other) % ny) * nx + (x + shift) % nx
    return pl.ds(pl.multiple_of(block * cols, cols), cols)


def columns_kernel(nx, ny, weight_ref, *refs):
    along_x, along_y, sem = refs[: nx - 1], refs[nx - 1], refs[nx]
    cols = along_y.shape[2]
    half = weight_ref.shape[0] // 2
    rows = pl.ds(pl.multiple_of(lax.axis_index("core") * half, half), half)
    sources, targets = [], []
    for s in range(1, nx):
        for o in range(ny):
            sources.append(weight_ref.at[rows, block_columns(nx, ny, s, o, cols)])
            targets.append(along_x[s - 1].at[o])
    for s in range(nx):
        sources.append(weight_ref.at[rows, block_columns(nx, ny, s, 1, cols)])
        targets.append(along_y.at[s])
    for c in fetch(sources, targets, sem):
        c.wait()


def stage_kernel(nx, ny, blocks, weight_ref, *refs):
    count = (len(refs) - 2) // 2
    came, own_ref, outs, sem = refs[:count], refs[count], refs[count + 1 : -1], refs[-1]
    cols = own_ref.shape[2]
    sources = [weight_ref.at[:, block_columns(nx, ny, s, o, cols)] for s, o in blocks]
    targets = [own_ref.at[i] for i in range(len(blocks))]
    for c in fetch(sources + list(came), targets + list(outs), sem):
        c.wait()


def core_halves(width):
    half = width // 2
    core = lax.axis_index("core")
    return [pl.ds(pl.multiple_of(c * half, half), half) for c in (core, 1 - core)]


def sums_over_x(other, pieces, weights):
    mine, rest = core_halves(pieces[0].shape[1])
    total = mm(pieces[0][...], weights[0][other])
    for s, piece in enumerate(pieces[1:]):
        total = total + mm(piece[:, mine], weights[1 + 2 * s][other])
        total = total + mm(piece[:, rest], weights[2 + 2 * s][other])
    return total


def sums_over_y(shift, pieces, weights):
    mine, rest = core_halves(pieces[0].shape[1])
    total = mm(pieces[0][...], weights[0][shift])
    return total + (mm(pieces[1][:, mine], weights[1][shift]) + mm(pieces[1][:, rest], weights[2][shift]))


def along_x_kernel(*refs):
    pieces, weights, outs = refs[:2], refs[2:5], refs[5:]
    for s, out_ref in enumerate(outs):
        out_ref[...] = sums_over_y(s + 1, pieces, weights).astype(out_ref.dtype)


def along_y_kernel(*refs):
    refs[11][...] = sums_over_x(1, refs[:4], refs[4:11]).astype(refs[11].dtype)


def own_kernel(*refs):
    refs[16][...] = sums_over_x(0, refs[:4], refs[4:11])
    refs[17][...] = sums_over_y(0, refs[11:13], refs[13:16])


def finish_kernel(upper_ref, lower_ref, *refs):
    along_y, along_x, out_ref = refs[0], refs[1:-1], refs[-1]
    half = upper_ref.shape[0]
    out_ref[:half, :] = (upper_ref[...] + along_y[...].astype(f32)).astype(out_ref.dtype)
    total = lower_ref[...]
    for came in along_x:
        total = total + came[...].astype(f32)
    out_ref[half:, :] = total.astype(out_ref.dtype)


def ring(axis, shift):
    size = lax.axis_size(axis)
    return [(i, (i + shift) % size) for i in range(size)]


VM = pl.BlockSpec(memory_space=pltpu.VMEM)
HBM = pl.BlockSpec(memory_space=pltpu.HBM)


def held(*arrays):
    return [pltpu.VMEM(a.shape, a.dtype) for a in arrays] + [pltpu.SemaphoreType.DMA((len(arrays),))]


def call(kernel, outs, scratch, flops, *args, specs=None, outs_at=VM):
    specs = specs or [VM] * len(args)
    args = [pltpu.with_memory_space_constraint(a, pltpu.HBM) if s is HBM else a for a, s in zip(args, specs)]
    moved = sum(a.size * a.dtype.itemsize for a in args)
    shapes = [jax.ShapeDtypeStruct(*o) for o in outs]
    result = pl.pallas_call(
        kernel,
        out_shape=shapes,
        in_specs=specs,
        out_specs=[outs_at] * len(shapes),
        scratch_shapes=scratch,
        compiler_params=pltpu.CompilerParams(vmem_limit_bytes=LIMIT),
        cost_estimate=pl.CostEstimate(flops=flops, bytes_accessed=moved, transcendentals=0),
    )(*args)
    return result if len(shapes) > 1 else result[0]


def transform(long_filter, fwd1, fwd2, twist):
    mine = long_filter.shape[1]
    rows = [pltpu.VMEM((SIDE * mine, SIDE), f32)]
    return call(filter_kernel, [((mine, SIDE, 2 * SIDE), f32)], rows, 10**9, long_filter.T, fwd1, fwd2, twist)


def convolve(signal, spectrum, fwd1, fwd2, inv2, twist):
    mine = signal.shape[1]
    rows = [pltpu.VMEM((SIDE * mine, SIDE), f32)] * 2
    inside = [pltpu.VMEM(signal.shape, bf16)]
    kept = held(fwd1, twist, fwd2, spectrum, inv2)[:-1]
    sems = [pltpu.SemaphoreType.DMA((5,)), pltpu.SemaphoreType.DMA((4,))]
    return call(
        conv_kernel, [(signal.shape, bf16)], rows + inside + kept + sems, 3 * 10**9,
        signal, fwd1, twist, fwd2, spectrum, inv2, specs=[VM] + [HBM] * 5, outs_at=HBM,
    )


def body(proj, short_filter, long_filter, out_weight):
    tokens, _, width = proj.shape
    ctx = lax.axis_size(CTX)
    mine = width // ctx
    nx, ny = lax.axis_size("x"), lax.axis_size("yh")
    cols = out_weight.shape[1] // (nx * ny)
    fwd1, fwd2, inv2, twist = [jnp.asarray(t) for t in tables()]

    streams_first = jnp.transpose(proj, (1, 0, 2))
    edge = lax.ppermute(streams_first[:, tokens - EDGE :, :], CTX, [(i, i + 1) for i in range(ctx - 1)])
    ext = [pltpu.VMEM((tokens + EDGE, width), f32)]
    gated_in = call(
        gate_in_kernel, [((width, tokens), bf16)],
        ext
        + held(streams_first[1], streams_first[2], short_filter)[:-1]
        + [pltpu.VMEM((width, tokens), bf16), pltpu.SemaphoreType.DMA((9,)), pltpu.SemaphoreType.DMA((4,))],
        0, edge, streams_first, short_filter, specs=[VM, HBM, HBM], outs_at=HBM,
    )
    gated_in, out_weight = lax.optimization_barrier((gated_in, out_weight))
    signal = lax.all_to_all(gated_in.reshape(ctx, mine, tokens), CTX, 0, 0)

    def columns(*refs):
        columns_kernel(nx, ny, *refs)

    *along_x, along_y = call(
        columns,
        [((ny, width // 2, cols), bf16)] * (nx - 1) + [((nx, width // 2, cols), bf16)],
        [pltpu.SemaphoreType.DMA((ny * (nx - 1) + nx,))], 0, out_weight, specs=[HBM],
    )

    def swapped(block, axis, route):
        came = lax.ppermute(block, axis, route)
        return [came, lax.ppermute(came, "core", ring("core", 1))]

    across = ny * lax.axis_size("yl")
    for_upper, for_lower = [], swapped(along_y, ("yl", "yh"), [(i, across - 1 - i) for i in range(across)])
    for s in range(1, nx):
        for_upper += swapped(along_x[s - 1], "x", ring("x", s))

    spectrum = transform(long_filter, fwd1, fwd2, twist)
    convolved = convolve(signal, spectrum, fwd1, fwd2, inv2, twist)
    returned = lax.all_to_all(convolved, CTX, 0, 0).reshape(width, tokens)
    query = call(query_kernel, [((tokens, width), f32)], ext, 0, streams_first, edge, short_filter)
    half = tokens // 2
    upper, lower = call(gate_out_kernel, [((half, width), bf16)] * 2, [], 0, query, returned)

    def send(block, axis, shift):
        return lax.ppermute(block, axis, ring(axis, shift))

    def stage(blocks, came):
        def kernel(*refs):
            stage_kernel(nx, ny, blocks, *refs)

        shapes = [((len(blocks), width, cols), bf16)] + [(c.shape, bf16) for c in came]
        sems = [pltpu.SemaphoreType.DMA((len(blocks) + len(came),))]
        return call(kernel, shapes, sems, 0, out_weight, *came, specs=[HBM] * (1 + len(came)))

    lower_pieces = [lower, send(lower, "yh", 1)]
    upper_pieces = [upper] + [send(upper, "x", s) for s in range(1, nx)]
    for_lower = stage([(s, 0) for s in range(nx)], for_lower)
    sums = call(along_x_kernel, [((half, cols), bf16)] * (nx - 1), [], 10**9, *lower_pieces, *for_lower)
    summed_x = [send(sums[s - 1], "x", s) for s in range(1, nx)]
    for_upper = stage([(0, 0), (0, 1)], for_upper)
    sums = call(along_y_kernel, [((half, cols), bf16)], [], 10**9, *upper_pieces, *for_upper)
    summed_y = send(sums, "yh", 1)
    own = call(own_kernel, [((half, cols), f32)] * 2, [], 10**9, *upper_pieces, *for_upper, *lower_pieces, *for_lower)
    return call(finish_kernel, [((tokens, cols), bf16)], [], 0, *own, summed_y, *summed_x)


def solution(mesh):
    axes = Mesh(mesh.devices.reshape(8, 2, 2, 2, 4), ("z", "yl", "core", "yh", "x"))
    tp = ("yh", "x")
    placed = (P(CTX, None, tp), P(None, None, tp), P(None, tp + CTX), P(tp, None))
    return jax.shard_map(body, mesh=axes, in_specs=placed, out_specs=P(CTX, tp), check_vma=False)
```

```python
import jax
import jax.numpy as jnp
import numpy as np
from jax import lax
from jax.experimental import pallas as pl
from jax.experimental.pallas import tpu as pltpu
from jax.sharding import Mesh, PartitionSpec as P


CTX = ("z", "yl", "core")
SIDE = 128
LENGTH = SIDE * SIDE
EDGE = 8
LIMIT = 16 * 2**20
f32, bf16 = jnp.float32, jnp.bfloat16


def halves(table):
    high = table.astype(bf16)
    low = (table - high.astype(np.float64)).astype(bf16)
    return np.stack([high, low])


def tables():
    i = np.arange(SIDE)
    first = 2 * np.pi * np.outer(i + 0.25, i) / SIDE
    turn = 2 * np.pi * np.outer(i + 0.25, i) / LENGTH
    second = 2 * np.pi * np.outer(i, i) / SIDE
    c1, s1, c2, s2 = np.cos(first), np.sin(first), np.cos(second), np.sin(second)
    fwd1 = np.concatenate([c1, s1], 0)
    fwd2 = np.block([[c2, s2], [-s2, c2]])
    inv2 = np.concatenate([c1.T, s1.T], 1) / LENGTH
    twist = np.stack([np.cos(turn), np.sin(turn)]).astype(np.float32)
    return np.concatenate(halves(fwd1), 1), halves(fwd2), halves(inv2), twist


def split(x):
    high = x.astype(bf16)
    return high, (x - high.astype(f32)).astype(bf16)


def mm(a, b):
    return jnp.dot(a, b, preferred_element_type=f32)


def left3(tab, x):
    high, low = split(x)
    return mm(tab[0], high) + (mm(tab[1], high) + mm(tab[0], low))


def right3(x, tab):
    high, low = split(x)
    return mm(high, tab[0]) + (mm(low, tab[0]) + mm(high, tab[1]))


def stacked(first, twist):
    tc, ts = twist[0], twist[1]
    turned = []
    for w in range(first.shape[1] // SIDE):
        re, im = first[:SIDE, w * SIDE : (w + 1) * SIDE], first[SIDE:, w * SIDE : (w + 1) * SIDE]
        turned.append(jnp.concatenate([re * tc - im * ts, re * ts + im * tc], 1))
    return jnp.concatenate(turned, 0)


def filter_kernel(h_ref, fwd1_ref, fwd2_ref, twist_ref, out_ref, rows):
    channels = h_ref.shape[0]
    for n in range(SIDE):
        rows[n * channels : (n + 1) * channels, :] = h_ref[:, n * SIDE : (n + 1) * SIDE]

    group = jnp.concatenate([rows[pl.ds(w, SIDE, stride=channels), :] for w in range(channels)], 1)
    high, low = split(group)
    first = mm(fwd1_ref[...], jnp.concatenate([high, high], 0)) + mm(fwd1_ref[:, :SIDE], low)
    spectra = right3(stacked(first, twist_ref), fwd2_ref)
    for w in range(channels):
        out_ref[w] = spectra[w * SIDE : (w + 1) * SIDE]


def fetch(sources, targets, sem):
    copies = [pltpu.make_async_copy(a, b, sem.at[i]) for i, (a, b) in enumerate(zip(sources, targets))]
    for c in copies:
        c.start()
    return copies


def conv_kernel(u_ref, *refs):
    sources, out_hbm, rows, back, out_ref = refs[:5], refs[5], refs[6], refs[7], refs[8]
    held, sem, out_sem = refs[9:14], refs[14], refs[15]
    fwd1_ref, twist_ref, fwd2_ref, h_ref, inv2_ref = held
    copies = fetch(sources, held, sem)
    blocks, channels, local = u_ref.shape
    per = local // SIDE
    for i in range(blocks):
        for q in range(per):
            n = i * per + q
            rows[n * channels : (n + 1) * channels, :] = u_ref[i, :, q * SIDE : (q + 1) * SIDE].astype(f32)
    group = jnp.concatenate([rows[pl.ds(w, SIDE, stride=channels), :] for w in range(channels)], 1).astype(bf16)
    for c in copies[:3]:
        c.wait()
    first = mm(fwd1_ref[...], jnp.concatenate([group, group], 0))
    spectra = right3(stacked(first, twist_ref), fwd2_ref)
    for c in copies[3:]:
        c.wait()
    products = []
    for w in range(channels):
        s, h = spectra[w * SIDE : (w + 1) * SIDE], h_ref[w]
        sr, si, hr, hi = s[:, :SIDE], s[:, SIDE:], h[:, :SIDE], h[:, SIDE:]
        products.append(jnp.concatenate([sr * hr - si * hi, -(sr * hi + si * hr)], 1))
    b = right3(jnp.concatenate(products, 0), fwd2_ref)
    tc, ts = twist_ref[0], twist_ref[1]
    turned = []
    for w in range(channels):
        br, bi = b[w * SIDE : (w + 1) * SIDE, :SIDE], b[w * SIDE : (w + 1) * SIDE, SIDE:]
        turned.append(jnp.concatenate([br * tc - bi * ts, -(bi * tc + br * ts)], 0))
    y = left3(inv2_ref, jnp.concatenate(turned, 1))
    for w in range(channels):
        back[pl.ds(w, SIDE, stride=channels), :] = y[:, w * SIDE : (w + 1) * SIDE]
    outs = []
    for i in range(blocks):
        for q in range(per):
            n = i * per + q
            out_ref[i, :, q * SIDE : (q + 1) * SIDE] = back[n * channels : (n + 1) * channels, :].astype(bf16)
        if (i + 1) % (blocks // 4) == 0:
            at = pl.ds(i + 1 - blocks // 4, blocks // 4)
            outs.append(pltpu.make_async_copy(out_ref.at[at], out_hbm.at[at], out_sem.at[len(outs)]))
            outs[-1].start()
    for c in outs:
        c.wait()


def featured(x, edge_ref, taps_ref, ext, s, cut=slice(None)):
    tokens = x.shape[0]
    ext[EDGE : EDGE + tokens, cut] = x.astype(f32)
    ext[:EDGE, cut] = edge_ref[s, :, cut].astype(f32)
    total = taps_ref[s, 0:1, cut] * ext[EDGE : EDGE + tokens, cut]
    for j in range(1, taps_ref.shape[1]):
        total = total + taps_ref[s, j : j + 1, cut] * ext[EDGE - j : EDGE - j + tokens, cut]
    return total


def load_kernel(x_hbm, taps_hbm, keys_ref, values_ref, taps_ref, sem):
    for c in fetch((taps_hbm, x_hbm.at[1], x_hbm.at[2]), (taps_ref, keys_ref, values_ref), sem):
        c.wait()


def gate_in_kernel(edge_ref, keys_ref, values_ref, taps_ref, out_hbm, ext, out_ref, sem):
    parts = 4
    size = keys_ref.shape[1] // parts
    outs = []
    for p in range(parts):
        cut = slice(p * size, (p + 1) * size)
        key = featured(keys_ref[:, cut], edge_ref, taps_ref, ext, 1, cut)
        product = key * featured(values_ref[:, cut], edge_ref, taps_ref, ext, 2, cut)
        out_ref[cut, :] = product.T.astype(bf16)
        outs.append(pltpu.make_async_copy(out_ref.at[cut], out_hbm.at[cut], sem.at[p]))
        outs[-1].start()
    for c in outs:
        c.wait()


def query_kernel(x_ref, edge_ref, taps_ref, out_ref, ext):
    out_ref[...] = featured(x_ref[0], edge_ref, taps_ref, ext, 0)


def gate_out_kernel(query_ref, conv_ref, upper_ref, lower_ref):
    gated = (query_ref[...] * conv_ref[...].astype(f32).T).astype(bf16)
    half = upper_ref.shape[0]
    upper_ref[...] = gated[:half]
    lower_ref[...] = gated[half:]


def block_columns(nx, ny, shift, other, cols):
    x, yh = lax.axis_index("x"), lax.axis_index("yh")
    block = ((yh + other) % ny) * nx + (x + shift) % nx
    return pl.ds(pl.multiple_of(block * cols, cols), cols)


def columns_kernel(nx, ny, weight_ref, *refs):
    along_x, along_y, sem = refs[: nx - 1], refs[nx - 1], refs[nx]
    cols = along_y.shape[2]
    half = weight_ref.shape[0] // 2
    rows = pl.ds(pl.multiple_of(lax.axis_index("core") * half, half), half)
    sources, targets = [], []
    for s in range(1, nx):
        for o in range(ny):
            sources.append(weight_ref.at[rows, block_columns(nx, ny, s, o, cols)])
            targets.append(along_x[s - 1].at[o])
    for s in range(nx):
        sources.append(weight_ref.at[rows, block_columns(nx, ny, s, 1, cols)])
        targets.append(along_y.at[s])
    for c in fetch(sources, targets, sem):
        c.wait()


def stage_kernel(nx, ny, blocks, weight_ref, *refs):
    count = (len(refs) - 2) // 2
    came, own_ref, outs, sem = refs[:count], refs[count], refs[count + 1 : -1], refs[-1]
    cols = own_ref.shape[2]
    sources = [weight_ref.at[:, block_columns(nx, ny, s, o, cols)] for s, o in blocks]
    targets = [own_ref.at[i] for i in range(len(blocks))]
    for c in fetch(sources + list(came), targets + list(outs), sem):
        c.wait()


def core_halves(width):
    half = width // 2
    core = lax.axis_index("core")
    return [pl.ds(pl.multiple_of(c * half, half), half) for c in (core, 1 - core)]


def sums_over_x(other, pieces, weights):
    mine, rest = core_halves(pieces[0].shape[1])
    total = mm(pieces[0][...], weights[0][other])
    for s, piece in enumerate(pieces[1:]):
        total = total + mm(piece[:, mine], weights[1 + 2 * s][other])
        total = total + mm(piece[:, rest], weights[2 + 2 * s][other])
    return total


def sums_over_y(shift, pieces, weights):
    mine, rest = core_halves(pieces[0].shape[1])
    total = mm(pieces[0][...], weights[0][shift])
    return total + (mm(pieces[1][:, mine], weights[1][shift]) + mm(pieces[1][:, rest], weights[2][shift]))


def along_x_kernel(*refs):
    pieces, weights, outs = refs[:2], refs[2:5], refs[5:]
    for s, out_ref in enumerate(outs):
        out_ref[...] = sums_over_y(s + 1, pieces, weights).astype(out_ref.dtype)


def along_y_kernel(*refs):
    refs[11][...] = sums_over_x(1, refs[:4], refs[4:11]).astype(refs[11].dtype)


def own_kernel(*refs):
    refs[16][...] = sums_over_x(0, refs[:4], refs[4:11])
    refs[17][...] = sums_over_y(0, refs[11:13], refs[13:16])


def finish_kernel(upper_ref, lower_ref, *refs):
    along_y, along_x, out_ref = refs[0], refs[1:-1], refs[-1]
    half = upper_ref.shape[0]
    out_ref[:half, :] = (upper_ref[...] + along_y[...].astype(f32)).astype(out_ref.dtype)
    total = lower_ref[...]
    for came in along_x:
        total = total + came[...].astype(f32)
    out_ref[half:, :] = total.astype(out_ref.dtype)


def ring(axis, shift):
    size = lax.axis_size(axis)
    return [(i, (i + shift) % size) for i in range(size)]


VM = pl.BlockSpec(memory_space=pltpu.VMEM)
HBM = pl.BlockSpec(memory_space=pltpu.HBM)


def held(*arrays):
    return [pltpu.VMEM(a.shape, a.dtype) for a in arrays] + [pltpu.SemaphoreType.DMA((len(arrays),))]


def call(kernel, outs, scratch, flops, *args, specs=None, outs_at=VM):
    specs = specs or [VM] * len(args)
    args = [pltpu.with_memory_space_constraint(a, pltpu.HBM) if s is HBM else a for a, s in zip(args, specs)]
    moved = sum(a.size * a.dtype.itemsize for a in args)
    shapes = [jax.ShapeDtypeStruct(*o) for o in outs]
    result = pl.pallas_call(
        kernel,
        out_shape=shapes,
        in_specs=specs,
        out_specs=[outs_at] * len(shapes),
        scratch_shapes=scratch,
        compiler_params=pltpu.CompilerParams(vmem_limit_bytes=LIMIT),
        cost_estimate=pl.CostEstimate(flops=flops, bytes_accessed=moved, transcendentals=0),
    )(*args)
    return result if len(shapes) > 1 else result[0]


def transform(long_filter, fwd1, fwd2, twist):
    mine = long_filter.shape[1]
    rows = [pltpu.VMEM((SIDE * mine, SIDE), f32)]
    return call(filter_kernel, [((mine, SIDE, 2 * SIDE), f32)], rows, 10**9, long_filter.T, fwd1, fwd2, twist)


def convolve(signal, spectrum, fwd1, fwd2, inv2, twist):
    mine = signal.shape[1]
    rows = [pltpu.VMEM((SIDE * mine, SIDE), f32)] * 2
    inside = [pltpu.VMEM(signal.shape, bf16)]
    kept = held(fwd1, twist, fwd2, spectrum, inv2)[:-1]
    sems = [pltpu.SemaphoreType.DMA((5,)), pltpu.SemaphoreType.DMA((4,))]
    return call(
        conv_kernel, [(signal.shape, bf16)], rows + inside + kept + sems, 3 * 10**9,
        signal, fwd1, twist, fwd2, spectrum, inv2, specs=[VM] + [HBM] * 5, outs_at=HBM,
    )


def body(proj, short_filter, long_filter, out_weight):
    tokens, _, width = proj.shape
    ctx = lax.axis_size(CTX)
    mine = width // ctx
    nx, ny = lax.axis_size("x"), lax.axis_size("yh")
    cols = out_weight.shape[1] // (nx * ny)
    fwd1, fwd2, inv2, twist = [jnp.asarray(t) for t in tables()]

    streams_first = jnp.transpose(proj, (1, 0, 2))
    edge = lax.ppermute(streams_first[:, tokens - EDGE :, :], CTX, [(i, i + 1) for i in range(ctx - 1)])
    loaded = call(
        load_kernel, [((tokens, width), bf16)] * 2 + [(short_filter.shape, f32)],
        [pltpu.SemaphoreType.DMA((3,))], 0, streams_first, short_filter, specs=[HBM] * 2,
    )
    ext = [pltpu.VMEM((tokens + EDGE, width), f32)]
    gated_in = call(
        gate_in_kernel, [((width, tokens), bf16)],
        ext + [pltpu.VMEM((width, tokens), bf16), pltpu.SemaphoreType.DMA((4,))],
        0, edge, *loaded, outs_at=HBM,
    )
    gated_in, out_weight = lax.optimization_barrier((gated_in, out_weight))
    signal = lax.all_to_all(gated_in.reshape(ctx, mine, tokens), CTX, 0, 0)

    def columns(*refs):
        columns_kernel(nx, ny, *refs)

    *along_x, along_y = call(
        columns,
        [((ny, width // 2, cols), bf16)] * (nx - 1) + [((nx, width // 2, cols), bf16)],
        [pltpu.SemaphoreType.DMA((ny * (nx - 1) + nx,))], 0, out_weight, specs=[HBM],
    )

    def swapped(block, axis, route):
        came = lax.ppermute(block, axis, route)
        return [came, lax.ppermute(came, "core", ring("core", 1))]

    across = ny * lax.axis_size("yl")
    for_upper, for_lower = [], swapped(along_y, ("yl", "yh"), [(i, across - 1 - i) for i in range(across)])
    for s in range(1, nx):
        for_upper += swapped(along_x[s - 1], "x", ring("x", s))

    spectrum = transform(long_filter, fwd1, fwd2, twist)
    convolved = convolve(signal, spectrum, fwd1, fwd2, inv2, twist)
    returned = lax.all_to_all(convolved, CTX, 0, 0).reshape(width, tokens)
    query = call(query_kernel, [((tokens, width), f32)], ext, 0, streams_first, edge, short_filter)
    half = tokens // 2
    upper, lower = call(gate_out_kernel, [((half, width), bf16)] * 2, [], 0, query, returned)

    def send(block, axis, shift):
        return lax.ppermute(block, axis, ring(axis, shift))

    def stage(blocks, came):
        def kernel(*refs):
            stage_kernel(nx, ny, blocks, *refs)

        shapes = [((len(blocks), width, cols), bf16)] + [(c.shape, bf16) for c in came]
        sems = [pltpu.SemaphoreType.DMA((len(blocks) + len(came),))]
        return call(kernel, shapes, sems, 0, out_weight, *came, specs=[HBM] * (1 + len(came)))

    lower_pieces = [lower, send(lower, "yh", 1)]
    upper_pieces = [upper] + [send(upper, "x", s) for s in range(1, nx)]
    for_lower = stage([(s, 0) for s in range(nx)], for_lower)
    sums = call(along_x_kernel, [((half, cols), bf16)] * (nx - 1), [], 10**9, *lower_pieces, *for_lower)
    summed_x = [send(sums[s - 1], "x", s) for s in range(1, nx)]
    for_upper = stage([(0, 0), (0, 1)], for_upper)
    sums = call(along_y_kernel, [((half, cols), bf16)], [], 10**9, *upper_pieces, *for_upper)
    summed_y = send(sums, "yh", 1)
    own = call(own_kernel, [((half, cols), f32)] * 2, [], 10**9, *upper_pieces, *for_upper, *lower_pieces, *for_lower)
    return call(finish_kernel, [((tokens, cols), bf16)], [], 0, *own, summed_y, *summed_x)


def solution(mesh):
    axes = Mesh(mesh.devices.reshape(8, 2, 2, 2, 4), ("z", "yl", "core", "yh", "x"))
    tp = ("yh", "x")
    placed = (P(CTX, None, tp), P(None, None, tp), P(None, tp + CTX), P(tp, None))
    return jax.shard_map(body, mesh=axes, in_specs=placed, out_specs=P(CTX, tp), check_vma=False)
```

```python
import jax
import jax.numpy as jnp
import numpy as np
from jax import lax
from jax.experimental import pallas as pl
from jax.experimental.pallas import tpu as pltpu
from jax.sharding import Mesh, PartitionSpec as P


CTX = ("z", "yl", "core")
SIDE = 128
LENGTH = SIDE * SIDE
EDGE = 8
GROUPS = 4
LIMIT = 16 * 2**20
f32, bf16 = jnp.float32, jnp.bfloat16


def halves(table):
    high = table.astype(bf16)
    low = (table - high.astype(np.float64)).astype(bf16)
    return np.stack([high, low])


def tables():
    i = np.arange(SIDE)
    first = 2 * np.pi * np.outer(i + 0.25, i) / SIDE
    turn = 2 * np.pi * np.outer(i + 0.25, i) / LENGTH
    second = 2 * np.pi * np.outer(i, i) / SIDE
    c1, s1, c2, s2 = np.cos(first), np.sin(first), np.cos(second), np.sin(second)
    fwd1 = np.concatenate([c1, s1], 0)
    fwd2 = np.block([[c2, s2], [-s2, c2]])
    inv2 = np.concatenate([c1.T, s1.T], 1) / LENGTH
    twist = np.stack([np.cos(turn), np.sin(turn)]).astype(np.float32)
    return np.concatenate(halves(fwd1), 1), halves(fwd2), halves(inv2), twist


def split(x):
    high = x.astype(bf16)
    return high, (x - high.astype(f32)).astype(bf16)


def mm(a, b):
    return jnp.dot(a, b, preferred_element_type=f32)


def left3(tab, x):
    high, low = split(x)
    return mm(tab[0], high) + (mm(tab[1], high) + mm(tab[0], low))


def right3(x, tab):
    high, low = split(x)
    return mm(high, tab[0]) + (mm(low, tab[0]) + mm(high, tab[1]))


def stacked(first, twist):
    tc, ts = twist[0], twist[1]
    turned = []
    for w in range(first.shape[1] // SIDE):
        re, im = first[:SIDE, w * SIDE : (w + 1) * SIDE], first[SIDE:, w * SIDE : (w + 1) * SIDE]
        turned.append(jnp.concatenate([re * tc - im * ts, re * ts + im * tc], 1))
    return jnp.concatenate(turned, 0)


def filter_kernel(h_ref, fwd1_ref, fwd2_ref, twist_ref, out_ref, rows):
    channels = h_ref.shape[0]
    for n in range(SIDE):
        rows[n * channels : (n + 1) * channels, :] = h_ref[:, n * SIDE : (n + 1) * SIDE]

    group = jnp.concatenate([rows[pl.ds(w, SIDE, stride=channels), :] for w in range(channels)], 1)
    high, low = split(group)
    first = mm(fwd1_ref[...], jnp.concatenate([high, high], 0)) + mm(fwd1_ref[:, :SIDE], low)
    spectra = right3(stacked(first, twist_ref), fwd2_ref)
    for w in range(channels):
        out_ref[w] = spectra[w * SIDE : (w + 1) * SIDE]


def fetch(sources, targets, sem):
    copies = [pltpu.make_async_copy(a, b, sem.at[i]) for i, (a, b) in enumerate(zip(sources, targets))]
    for c in copies:
        c.start()
    return copies


def conv_kernel(u_ref, *refs):
    sources, out_hbm, rows, back, out_ref = refs[:5], refs[5], refs[6], refs[7], refs[8]
    held, sem, out_sem = refs[9:14], refs[14], refs[15]
    fwd1_ref, twist_ref, fwd2_ref, h_ref, inv2_ref = held
    copies = fetch(sources, held, sem)
    blocks, channels, local = u_ref.shape
    per = local // SIDE
    for i in range(blocks):
        for q in range(per):
            n = i * per + q
            rows[n * channels : (n + 1) * channels, :] = u_ref[i, :, q * SIDE : (q + 1) * SIDE].astype(f32)
    size = channels // GROUPS
    groups = [range(g * size, (g + 1) * size) for g in range(GROUPS)]
    signals = [
        jnp.concatenate([rows[pl.ds(w, SIDE, stride=channels), :] for w in group], 1).astype(bf16) for group in groups
    ]
    for c in copies[:3]:
        c.wait()
    firsts = [mm(fwd1_ref[...], jnp.concatenate([x, x], 0)) for x in signals]
    turned = [stacked(first, twist_ref) for first in firsts]
    spectra = [right3(x, fwd2_ref) for x in turned]
    for c in copies[3:]:
        c.wait()
    products = []
    for group, spectrum in zip(groups, spectra):
        parts = []
        for w, channel in enumerate(group):
            s, h = spectrum[w * SIDE : (w + 1) * SIDE], h_ref[channel]
            sr, si, hr, hi = s[:, :SIDE], s[:, SIDE:], h[:, :SIDE], h[:, SIDE:]
            parts.append(jnp.concatenate([sr * hr - si * hi, -(sr * hi + si * hr)], 1))
        products.append(jnp.concatenate(parts, 0))
    tc, ts = twist_ref[0], twist_ref[1]
    backs = [right3(x, fwd2_ref) for x in products]
    results = []
    for b in backs:
        parts = []
        for w in range(size):
            br, bi = b[w * SIDE : (w + 1) * SIDE, :SIDE], b[w * SIDE : (w + 1) * SIDE, SIDE:]
            parts.append(jnp.concatenate([br * tc - bi * ts, -(bi * tc + br * ts)], 0))
        results.append(jnp.concatenate(parts, 1))
    results = [left3(inv2_ref, x) for x in results]
    for group, y in zip(groups, results):
        for w, channel in enumerate(group):
            back[pl.ds(channel, SIDE, stride=channels), :] = y[:, w * SIDE : (w + 1) * SIDE]
    outs = []
    for i in range(blocks):
        for q in range(per):
            n = i * per + q
            out_ref[i, :, q * SIDE : (q + 1) * SIDE] = back[n * channels : (n + 1) * channels, :].astype(bf16)
        if (i + 1) % (blocks // 4) == 0:
            at = pl.ds(i + 1 - blocks // 4, blocks // 4)
            outs.append(pltpu.make_async_copy(out_ref.at[at], out_hbm.at[at], out_sem.at[len(outs)]))
            outs[-1].start()
    for c in outs:
        c.wait()


def featured(x, edge_ref, taps_ref, ext, s, cut=slice(None)):
    tokens = x.shape[0]
    ext[EDGE : EDGE + tokens, cut] = x.astype(f32)
    ext[:EDGE, cut] = edge_ref[s, :, cut].astype(f32)
    total = taps_ref[s, 0:1, cut] * ext[EDGE : EDGE + tokens, cut]
    for j in range(1, taps_ref.shape[1]):
        total = total + taps_ref[s, j : j + 1, cut] * ext[EDGE - j : EDGE - j + tokens, cut]
    return total


def load_kernel(x_hbm, taps_hbm, keys_ref, values_ref, taps_ref, sem):
    for c in fetch((taps_hbm, x_hbm.at[1], x_hbm.at[2]), (taps_ref, keys_ref, values_ref), sem):
        c.wait()


def gate_in_kernel(edge_ref, keys_ref, values_ref, taps_ref, out_hbm, ext, out_ref, sem):
    parts = 4
    size = keys_ref.shape[1] // parts
    outs = []
    for p in range(parts):
        cut = slice(p * size, (p + 1) * size)
        key = featured(keys_ref[:, cut], edge_ref, taps_ref, ext, 1, cut)
        product = key * featured(values_ref[:, cut], edge_ref, taps_ref, ext, 2, cut)
        out_ref[cut, :] = product.T.astype(bf16)
        outs.append(pltpu.make_async_copy(out_ref.at[cut], out_hbm.at[cut], sem.at[p]))
        outs[-1].start()
    for c in outs:
        c.wait()


def query_kernel(x_ref, edge_ref, taps_ref, out_ref, ext):
    out_ref[...] = featured(x_ref[0], edge_ref, taps_ref, ext, 0)


def gate_out_kernel(query_ref, conv_ref, upper_ref, lower_ref):
    gated = (query_ref[...] * conv_ref[...].astype(f32).T).astype(bf16)
    half = upper_ref.shape[0]
    upper_ref[...] = gated[:half]
    lower_ref[...] = gated[half:]


def block_columns(nx, ny, shift, other, cols):
    x, yh = lax.axis_index("x"), lax.axis_index("yh")
    block = ((yh + other) % ny) * nx + (x + shift) % nx
    return pl.ds(pl.multiple_of(block * cols, cols), cols)


def columns_kernel(nx, ny, weight_ref, *refs):
    along_x, along_y, sem = refs[: nx - 1], refs[nx - 1], refs[nx]
    cols = along_y.shape[2]
    half = weight_ref.shape[0] // 2
    rows = pl.ds(pl.multiple_of(lax.axis_index("core") * half, half), half)
    sources, targets = [], []
    for s in range(1, nx):
        for o in range(ny):
            sources.append(weight_ref.at[rows, block_columns(nx, ny, s, o, cols)])
            targets.append(along_x[s - 1].at[o])
    for s in range(nx):
        sources.append(weight_ref.at[rows, block_columns(nx, ny, s, 1, cols)])
        targets.append(along_y.at[s])
    for c in fetch(sources, targets, sem):
        c.wait()


def stage_kernel(nx, ny, blocks, weight_ref, *refs):
    count = (len(refs) - 2) // 2
    came, own_ref, outs, sem = refs[:count], refs[count], refs[count + 1 : -1], refs[-1]
    cols = own_ref.shape[2]
    sources = [weight_ref.at[:, block_columns(nx, ny, s, o, cols)] for s, o in blocks]
    targets = [own_ref.at[i] for i in range(len(blocks))]
    for c in fetch(sources + list(came), targets + list(outs), sem):
        c.wait()


def core_halves(width):
    half = width // 2
    core = lax.axis_index("core")
    return [pl.ds(pl.multiple_of(c * half, half), half) for c in (core, 1 - core)]


def sums_over_x(other, pieces, weights):
    mine, rest = core_halves(pieces[0].shape[1])
    total = mm(pieces[0][...], weights[0][other])
    for s, piece in enumerate(pieces[1:]):
        total = total + mm(piece[:, mine], weights[1 + 2 * s][other])
        total = total + mm(piece[:, rest], weights[2 + 2 * s][other])
    return total


def sums_over_y(shift, pieces, weights):
    mine, rest = core_halves(pieces[0].shape[1])
    total = mm(pieces[0][...], weights[0][shift])
    return total + (mm(pieces[1][:, mine], weights[1][shift]) + mm(pieces[1][:, rest], weights[2][shift]))


def along_x_kernel(*refs):
    pieces, weights, outs = refs[:2], refs[2:5], refs[5:]
    for s, out_ref in enumerate(outs):
        out_ref[...] = sums_over_y(s + 1, pieces, weights).astype(out_ref.dtype)


def along_y_kernel(*refs):
    refs[11][...] = sums_over_x(1, refs[:4], refs[4:11]).astype(refs[11].dtype)


def own_kernel(*refs):
    refs[16][...] = sums_over_x(0, refs[:4], refs[4:11])
    refs[17][...] = sums_over_y(0, refs[11:13], refs[13:16])


def finish_kernel(upper_ref, lower_ref, *refs):
    along_y, along_x, out_ref = refs[0], refs[1:-1], refs[-1]
    half = upper_ref.shape[0]
    out_ref[:half, :] = (upper_ref[...] + along_y[...].astype(f32)).astype(out_ref.dtype)
    total = lower_ref[...]
    for came in along_x:
        total = total + came[...].astype(f32)
    out_ref[half:, :] = total.astype(out_ref.dtype)


def ring(axis, shift):
    size = lax.axis_size(axis)
    return [(i, (i + shift) % size) for i in range(size)]


VM = pl.BlockSpec(memory_space=pltpu.VMEM)
HBM = pl.BlockSpec(memory_space=pltpu.HBM)


def held(*arrays):
    return [pltpu.VMEM(a.shape, a.dtype) for a in arrays] + [pltpu.SemaphoreType.DMA((len(arrays),))]


def call(kernel, outs, scratch, flops, *args, specs=None, outs_at=VM):
    specs = specs or [VM] * len(args)
    args = [pltpu.with_memory_space_constraint(a, pltpu.HBM) if s is HBM else a for a, s in zip(args, specs)]
    moved = sum(a.size * a.dtype.itemsize for a in args)
    shapes = [jax.ShapeDtypeStruct(*o) for o in outs]
    result = pl.pallas_call(
        kernel,
        out_shape=shapes,
        in_specs=specs,
        out_specs=[outs_at] * len(shapes),
        scratch_shapes=scratch,
        compiler_params=pltpu.CompilerParams(vmem_limit_bytes=LIMIT),
        cost_estimate=pl.CostEstimate(flops=flops, bytes_accessed=moved, transcendentals=0),
    )(*args)
    return result if len(shapes) > 1 else result[0]


def transform(long_filter, fwd1, fwd2, twist):
    mine = long_filter.shape[1]
    rows = [pltpu.VMEM((SIDE * mine, SIDE), f32)]
    return call(filter_kernel, [((mine, SIDE, 2 * SIDE), f32)], rows, 10**9, long_filter.T, fwd1, fwd2, twist)


def convolve(signal, spectrum, fwd1, fwd2, inv2, twist):
    mine = signal.shape[1]
    rows = [pltpu.VMEM((SIDE * mine, SIDE), f32)] * 2
    inside = [pltpu.VMEM(signal.shape, bf16)]
    kept = held(fwd1, twist, fwd2, spectrum, inv2)[:-1]
    sems = [pltpu.SemaphoreType.DMA((5,)), pltpu.SemaphoreType.DMA((4,))]
    return call(
        conv_kernel, [(signal.shape, bf16)], rows + inside + kept + sems, 3 * 10**9,
        signal, fwd1, twist, fwd2, spectrum, inv2, specs=[VM] + [HBM] * 5, outs_at=HBM,
    )


def body(proj, short_filter, long_filter, out_weight):
    tokens, _, width = proj.shape
    ctx = lax.axis_size(CTX)
    mine = width // ctx
    nx, ny = lax.axis_size("x"), lax.axis_size("yh")
    cols = out_weight.shape[1] // (nx * ny)
    fwd1, fwd2, inv2, twist = [jnp.asarray(t) for t in tables()]

    streams_first = jnp.transpose(proj, (1, 0, 2))
    edge = lax.ppermute(streams_first[:, tokens - EDGE :, :], CTX, [(i, i + 1) for i in range(ctx - 1)])
    loaded = call(
        load_kernel, [((tokens, width), bf16)] * 2 + [(short_filter.shape, f32)],
        [pltpu.SemaphoreType.DMA((3,))], 0, streams_first, short_filter, specs=[HBM] * 2,
    )
    ext = [pltpu.VMEM((tokens + EDGE, width), f32)]
    gated_in = call(
        gate_in_kernel, [((width, tokens), bf16)],
        ext + [pltpu.VMEM((width, tokens), bf16), pltpu.SemaphoreType.DMA((4,))],
        0, edge, *loaded, outs_at=HBM,
    )
    gated_in, out_weight = lax.optimization_barrier((gated_in, out_weight))
    signal = lax.all_to_all(gated_in.reshape(ctx, mine, tokens), CTX, 0, 0)

    def columns(*refs):
        columns_kernel(nx, ny, *refs)

    *along_x, along_y = call(
        columns,
        [((ny, width // 2, cols), bf16)] * (nx - 1) + [((nx, width // 2, cols), bf16)],
        [pltpu.SemaphoreType.DMA((ny * (nx - 1) + nx,))], 0, out_weight, specs=[HBM],
    )

    def swapped(block, axis, route):
        came = lax.ppermute(block, axis, route)
        return [came, lax.ppermute(came, "core", ring("core", 1))]

    across = ny * lax.axis_size("yl")
    for_upper, for_lower = [], swapped(along_y, ("yl", "yh"), [(i, across - 1 - i) for i in range(across)])
    for s in range(1, nx):
        for_upper += swapped(along_x[s - 1], "x", ring("x", s))

    spectrum = transform(long_filter, fwd1, fwd2, twist)
    convolved = convolve(signal, spectrum, fwd1, fwd2, inv2, twist)
    returned = lax.all_to_all(convolved, CTX, 0, 0).reshape(width, tokens)
    query = call(query_kernel, [((tokens, width), f32)], ext, 0, streams_first, edge, short_filter)
    half = tokens // 2
    upper, lower = call(gate_out_kernel, [((half, width), bf16)] * 2, [], 0, query, returned)

    def send(block, axis, shift):
        return lax.ppermute(block, axis, ring(axis, shift))

    def stage(blocks, came):
        def kernel(*refs):
            stage_kernel(nx, ny, blocks, *refs)

        shapes = [((len(blocks), width, cols), bf16)] + [(c.shape, bf16) for c in came]
        sems = [pltpu.SemaphoreType.DMA((len(blocks) + len(came),))]
        return call(kernel, shapes, sems, 0, out_weight, *came, specs=[HBM] * (1 + len(came)))

    lower_pieces = [lower, send(lower, "yh", 1)]
    upper_pieces = [upper] + [send(upper, "x", s) for s in range(1, nx)]
    for_lower = stage([(s, 0) for s in range(nx)], for_lower)
    sums = call(along_x_kernel, [((half, cols), bf16)] * (nx - 1), [], 10**9, *lower_pieces, *for_lower)
    summed_x = [send(sums[s - 1], "x", s) for s in range(1, nx)]
    for_upper = stage([(0, 0), (0, 1)], for_upper)
    sums = call(along_y_kernel, [((half, cols), bf16)], [], 10**9, *upper_pieces, *for_upper)
    summed_y = send(sums, "yh", 1)
    own = call(own_kernel, [((half, cols), f32)] * 2, [], 10**9, *upper_pieces, *for_upper, *lower_pieces, *for_lower)
    return call(finish_kernel, [((tokens, cols), bf16)], [], 0, *own, summed_y, *summed_x)


def solution(mesh):
    axes = Mesh(mesh.devices.reshape(8, 2, 2, 2, 4), ("z", "yl", "core", "yh", "x"))
    tp = ("yh", "x")
    placed = (P(CTX, None, tp), P(None, None, tp), P(None, tp + CTX), P(tp, None))
    return jax.shard_map(body, mesh=axes, in_specs=placed, out_specs=P(CTX, tp), check_vma=False)
```

```python
import jax
import jax.numpy as jnp
import numpy as np
from jax import lax
from jax.experimental import pallas as pl
from jax.experimental.pallas import tpu as pltpu
from jax.sharding import Mesh, PartitionSpec as P


CTX = ("z", "yl", "core")
SIDE = 128
LENGTH = SIDE * SIDE
EDGE = 8
GROUPS = 4
LIMIT = 16 * 2**20
f32, bf16 = jnp.float32, jnp.bfloat16


def halves(table):
    high = table.astype(bf16)
    low = (table - high.astype(np.float64)).astype(bf16)
    return np.stack([high, low])


def tables():
    i = np.arange(SIDE)
    first = 2 * np.pi * np.outer(i + 0.25, i) / SIDE
    turn = 2 * np.pi * np.outer(i + 0.25, i) / LENGTH
    second = 2 * np.pi * np.outer(i, i) / SIDE
    c1, s1, c2, s2 = np.cos(first), np.sin(first), np.cos(second), np.sin(second)
    fwd1 = np.concatenate([c1, s1], 0)
    fwd2 = np.block([[c2, s2], [-s2, c2]])
    inv2 = np.concatenate([c1.T, s1.T], 1) / LENGTH
    twist = np.stack([np.cos(turn), np.sin(turn)]).astype(np.float32)
    return np.concatenate(halves(fwd1), 1), halves(fwd2), halves(inv2), twist


def split(x):
    high = x.astype(bf16)
    return high, (x - high.astype(f32)).astype(bf16)


def mm(a, b):
    return jnp.dot(a, b, preferred_element_type=f32)


def left3(tab, x):
    high, low = split(x)
    return mm(tab[0], high) + (mm(tab[1], high) + mm(tab[0], low))


def right3(x, tab):
    high, low = split(x)
    return mm(high, tab[0]) + (mm(low, tab[0]) + mm(high, tab[1]))


def stacked(first, twist):
    tc, ts = twist[0], twist[1]
    turned = []
    for w in range(first.shape[1] // SIDE):
        re, im = first[:SIDE, w * SIDE : (w + 1) * SIDE], first[SIDE:, w * SIDE : (w + 1) * SIDE]
        turned.append(jnp.concatenate([re * tc - im * ts, re * ts + im * tc], 1))
    return jnp.concatenate(turned, 0)


def filter_kernel(h_ref, fwd1_ref, fwd2_ref, twist_ref, out_ref, rows):
    channels = h_ref.shape[0]
    for n in range(SIDE):
        rows[n * channels : (n + 1) * channels, :] = h_ref[:, n * SIDE : (n + 1) * SIDE]

    group = jnp.concatenate([rows[pl.ds(w, SIDE, stride=channels), :] for w in range(channels)], 1)
    high, low = split(group)
    first = mm(fwd1_ref[...], jnp.concatenate([high, high], 0)) + mm(fwd1_ref[:, :SIDE], low)
    spectra = right3(stacked(first, twist_ref), fwd2_ref)
    for w in range(channels):
        out_ref[w] = spectra[w * SIDE : (w + 1) * SIDE]


def fetch(sources, targets, sem):
    copies = [pltpu.make_async_copy(a, b, sem.at[i]) for i, (a, b) in enumerate(zip(sources, targets))]
    for c in copies:
        c.start()
    return copies


def conv_kernel(u_ref, *refs):
    sources, out_hbm, rows, back, out_ref = refs[:5], refs[5], refs[6], refs[7], refs[8]
    held, sem, out_sem = refs[9:14], refs[14], refs[15]
    fwd1_ref, twist_ref, fwd2_ref, h_ref, inv2_ref = held
    copies = fetch(sources, held, sem)
    blocks, channels, local = u_ref.shape
    per = local // SIDE
    for i in range(blocks):
        for q in range(per):
            n = i * per + q
            rows[n * channels : (n + 1) * channels, :] = u_ref[i, :, q * SIDE : (q + 1) * SIDE].astype(f32)
    size = channels // GROUPS
    groups = [range(g * size, (g + 1) * size) for g in range(GROUPS)]
    signals = [
        jnp.concatenate([rows[pl.ds(w, SIDE, stride=channels), :] for w in group], 1).astype(bf16) for group in groups
    ]
    for c in copies[:3]:
        c.wait()
    firsts = [mm(fwd1_ref[...], jnp.concatenate([x, x], 0)) for x in signals]
    turned = [stacked(first, twist_ref) for first in firsts]
    spectra = [right3(x, fwd2_ref) for x in turned]
    for c in copies[3:]:
        c.wait()
    products = []
    for group, spectrum in zip(groups, spectra):
        parts = []
        for w, channel in enumerate(group):
            s, h = spectrum[w * SIDE : (w + 1) * SIDE], h_ref[channel]
            sr, si, hr, hi = s[:, :SIDE], s[:, SIDE:], h[:, :SIDE], h[:, SIDE:]
            parts.append(jnp.concatenate([sr * hr - si * hi, -(sr * hi + si * hr)], 1))
        products.append(jnp.concatenate(parts, 0))
    tc, ts = twist_ref[0], twist_ref[1]
    backs = [right3(x, fwd2_ref) for x in products]
    results = []
    for b in backs:
        parts = []
        for w in range(size):
            br, bi = b[w * SIDE : (w + 1) * SIDE, :SIDE], b[w * SIDE : (w + 1) * SIDE, SIDE:]
            parts.append(jnp.concatenate([br * tc - bi * ts, -(bi * tc + br * ts)], 0))
        results.append(jnp.concatenate(parts, 1))
    results = [left3(inv2_ref, x) for x in results]
    for group, y in zip(groups, results):
        for w, channel in enumerate(group):
            back[pl.ds(channel, SIDE, stride=channels), :] = y[:, w * SIDE : (w + 1) * SIDE]
    outs = []
    for i in range(blocks):
        for q in range(per):
            n = i * per + q
            out_ref[i, :, q * SIDE : (q + 1) * SIDE] = back[n * channels : (n + 1) * channels, :].astype(bf16)
        if (i + 1) % (blocks // 4) == 0:
            at = pl.ds(i + 1 - blocks // 4, blocks // 4)
            outs.append(pltpu.make_async_copy(out_ref.at[at], out_hbm.at[at], out_sem.at[len(outs)]))
            outs[-1].start()
    for c in outs:
        c.wait()


def featured(x, edge_ref, taps_ref, s, cut=slice(None)):
    whole = jnp.concatenate([edge_ref[s, :, cut].astype(f32), x.astype(f32)], 0)
    total = taps_ref[s, 0:1, cut] * whole[EDGE:]
    for j in range(1, taps_ref.shape[1]):
        total = total + taps_ref[s, j : j + 1, cut] * pltpu.roll(whole, j, 0)[EDGE:]
    return total


def load_kernel(x_hbm, taps_hbm, keys_ref, values_ref, taps_ref, sem):
    for c in fetch((taps_hbm, x_hbm.at[1], x_hbm.at[2]), (taps_ref, keys_ref, values_ref), sem):
        c.wait()


def gate_in_kernel(edge_ref, keys_ref, values_ref, taps_ref, out_hbm, out_ref, sem):
    parts = 4
    size = keys_ref.shape[1] // parts
    outs = []
    for p in range(parts):
        cut = slice(p * size, (p + 1) * size)
        key = featured(keys_ref[:, cut], edge_ref, taps_ref, 1, cut)
        product = key * featured(values_ref[:, cut], edge_ref, taps_ref, 2, cut)
        out_ref[cut, :] = product.T.astype(bf16)
        outs.append(pltpu.make_async_copy(out_ref.at[cut], out_hbm.at[cut], sem.at[p]))
        outs[-1].start()
    for c in outs:
        c.wait()


def query_kernel(x_ref, edge_ref, taps_ref, out_ref):
    out_ref[...] = featured(x_ref[0], edge_ref, taps_ref, 0)


def gate_out_kernel(query_ref, conv_ref, upper_ref, lower_ref):
    gated = (query_ref[...] * conv_ref[...].astype(f32).T).astype(bf16)
    half = upper_ref.shape[0]
    upper_ref[...] = gated[:half]
    lower_ref[...] = gated[half:]


def block_columns(nx, ny, shift, other, cols):
    x, yh = lax.axis_index("x"), lax.axis_index("yh")
    block = ((yh + other) % ny) * nx + (x + shift) % nx
    return pl.ds(pl.multiple_of(block * cols, cols), cols)


def columns_kernel(nx, ny, weight_ref, *refs):
    along_x, along_y, sem = refs[: nx - 1], refs[nx - 1], refs[nx]
    cols = along_y.shape[2]
    half = weight_ref.shape[0] // 2
    rows = pl.ds(pl.multiple_of(lax.axis_index("core") * half, half), half)
    sources, targets = [], []
    for s in range(1, nx):
        for o in range(ny):
            sources.append(weight_ref.at[rows, block_columns(nx, ny, s, o, cols)])
            targets.append(along_x[s - 1].at[o])
    for s in range(nx):
        sources.append(weight_ref.at[rows, block_columns(nx, ny, s, 1, cols)])
        targets.append(along_y.at[s])
    for c in fetch(sources, targets, sem):
        c.wait()


def stage_kernel(nx, ny, blocks, weight_ref, *refs):
    count = (len(refs) - 2) // 2
    came, own_ref, outs, sem = refs[:count], refs[count], refs[count + 1 : -1], refs[-1]
    cols = own_ref.shape[2]
    sources = [weight_ref.at[:, block_columns(nx, ny, s, o, cols)] for s, o in blocks]
    targets = [own_ref.at[i] for i in range(len(blocks))]
    for c in fetch(sources + list(came), targets + list(outs), sem):
        c.wait()


def core_halves(width):
    half = width // 2
    core = lax.axis_index("core")
    return [pl.ds(pl.multiple_of(c * half, half), half) for c in (core, 1 - core)]


def sums_over_x(other, pieces, weights):
    mine, rest = core_halves(pieces[0].shape[1])
    total = mm(pieces[0][...], weights[0][other])
    for s, piece in enumerate(pieces[1:]):
        total = total + mm(piece[:, mine], weights[1 + 2 * s][other])
        total = total + mm(piece[:, rest], weights[2 + 2 * s][other])
    return total


def sums_over_y(shift, pieces, weights):
    mine, rest = core_halves(pieces[0].shape[1])
    total = mm(pieces[0][...], weights[0][shift])
    return total + (mm(pieces[1][:, mine], weights[1][shift]) + mm(pieces[1][:, rest], weights[2][shift]))


def along_x_kernel(*refs):
    pieces, weights, outs = refs[:2], refs[2:5], refs[5:]
    for s, out_ref in enumerate(outs):
        out_ref[...] = sums_over_y(s + 1, pieces, weights).astype(out_ref.dtype)


def along_y_kernel(*refs):
    refs[11][...] = sums_over_x(1, refs[:4], refs[4:11]).astype(refs[11].dtype)


def own_kernel(*refs):
    refs[16][...] = sums_over_x(0, refs[:4], refs[4:11])
    refs[17][...] = sums_over_y(0, refs[11:13], refs[13:16])


def finish_kernel(upper_ref, lower_ref, *refs):
    along_y, along_x, out_ref = refs[0], refs[1:-1], refs[-1]
    half = upper_ref.shape[0]
    out_ref[:half, :] = (upper_ref[...] + along_y[...].astype(f32)).astype(out_ref.dtype)
    total = lower_ref[...]
    for came in along_x:
        total = total + came[...].astype(f32)
    out_ref[half:, :] = total.astype(out_ref.dtype)


def ring(axis, shift):
    size = lax.axis_size(axis)
    return [(i, (i + shift) % size) for i in range(size)]


VM = pl.BlockSpec(memory_space=pltpu.VMEM)
HBM = pl.BlockSpec(memory_space=pltpu.HBM)


def held(*arrays):
    return [pltpu.VMEM(a.shape, a.dtype) for a in arrays] + [pltpu.SemaphoreType.DMA((len(arrays),))]


def call(kernel, outs, scratch, flops, *args, specs=None, outs_at=VM):
    specs = specs or [VM] * len(args)
    args = [pltpu.with_memory_space_constraint(a, pltpu.HBM) if s is HBM else a for a, s in zip(args, specs)]
    moved = sum(a.size * a.dtype.itemsize for a in args)
    shapes = [jax.ShapeDtypeStruct(*o) for o in outs]
    result = pl.pallas_call(
        kernel,
        out_shape=shapes,
        in_specs=specs,
        out_specs=[outs_at] * len(shapes),
        scratch_shapes=scratch,
        compiler_params=pltpu.CompilerParams(vmem_limit_bytes=LIMIT),
        cost_estimate=pl.CostEstimate(flops=flops, bytes_accessed=moved, transcendentals=0),
    )(*args)
    return result if len(shapes) > 1 else result[0]


def transform(long_filter, fwd1, fwd2, twist):
    mine = long_filter.shape[1]
    rows = [pltpu.VMEM((SIDE * mine, SIDE), f32)]
    return call(filter_kernel, [((mine, SIDE, 2 * SIDE), f32)], rows, 10**9, long_filter.T, fwd1, fwd2, twist)


def convolve(signal, spectrum, fwd1, fwd2, inv2, twist):
    mine = signal.shape[1]
    rows = [pltpu.VMEM((SIDE * mine, SIDE), f32)] * 2
    inside = [pltpu.VMEM(signal.shape, bf16)]
    kept = held(fwd1, twist, fwd2, spectrum, inv2)[:-1]
    sems = [pltpu.SemaphoreType.DMA((5,)), pltpu.SemaphoreType.DMA((4,))]
    return call(
        conv_kernel, [(signal.shape, bf16)], rows + inside + kept + sems, 3 * 10**9,
        signal, fwd1, twist, fwd2, spectrum, inv2, specs=[VM] + [HBM] * 5, outs_at=HBM,
    )


def body(proj, short_filter, long_filter, out_weight):
    tokens, _, width = proj.shape
    ctx = lax.axis_size(CTX)
    mine = width // ctx
    nx, ny = lax.axis_size("x"), lax.axis_size("yh")
    cols = out_weight.shape[1] // (nx * ny)
    fwd1, fwd2, inv2, twist = [jnp.asarray(t) for t in tables()]

    streams_first = jnp.transpose(proj, (1, 0, 2))
    edge = lax.ppermute(streams_first[:, tokens - EDGE :, :], CTX, [(i, i + 1) for i in range(ctx - 1)])
    loaded = call(
        load_kernel, [((tokens, width), bf16)] * 2 + [(short_filter.shape, f32)],
        [pltpu.SemaphoreType.DMA((3,))], 0, streams_first, short_filter, specs=[HBM] * 2,
    )
    gated_in = call(
        gate_in_kernel, [((width, tokens), bf16)],
        [pltpu.VMEM((width, tokens), bf16), pltpu.SemaphoreType.DMA((4,))],
        0, edge, *loaded, outs_at=HBM,
    )
    gated_in, out_weight = lax.optimization_barrier((gated_in, out_weight))
    signal = lax.all_to_all(gated_in.reshape(ctx, mine, tokens), CTX, 0, 0)

    def columns(*refs):
        columns_kernel(nx, ny, *refs)

    *along_x, along_y = call(
        columns,
        [((ny, width // 2, cols), bf16)] * (nx - 1) + [((nx, width // 2, cols), bf16)],
        [pltpu.SemaphoreType.DMA((ny * (nx - 1) + nx,))], 0, out_weight, specs=[HBM],
    )

    def swapped(block, axis, route):
        came = lax.ppermute(block, axis, route)
        return [came, lax.ppermute(came, "core", ring("core", 1))]

    across = ny * lax.axis_size("yl")
    for_upper, for_lower = [], swapped(along_y, ("yl", "yh"), [(i, across - 1 - i) for i in range(across)])
    for s in range(1, nx):
        for_upper += swapped(along_x[s - 1], "x", ring("x", s))

    spectrum = transform(long_filter, fwd1, fwd2, twist)
    convolved = convolve(signal, spectrum, fwd1, fwd2, inv2, twist)
    returned = lax.all_to_all(convolved, CTX, 0, 0).reshape(width, tokens)
    query = call(query_kernel, [((tokens, width), f32)], [], 0, streams_first, edge, short_filter)
    half = tokens // 2
    upper, lower = call(gate_out_kernel, [((half, width), bf16)] * 2, [], 0, query, returned)

    def send(block, axis, shift):
        return lax.ppermute(block, axis, ring(axis, shift))

    def stage(blocks, came):
        def kernel(*refs):
            stage_kernel(nx, ny, blocks, *refs)

        shapes = [((len(blocks), width, cols), bf16)] + [(c.shape, bf16) for c in came]
        sems = [pltpu.SemaphoreType.DMA((len(blocks) + len(came),))]
        return call(kernel, shapes, sems, 0, out_weight, *came, specs=[HBM] * (1 + len(came)))

    lower_pieces = [lower, send(lower, "yh", 1)]
    upper_pieces = [upper] + [send(upper, "x", s) for s in range(1, nx)]
    for_lower = stage([(s, 0) for s in range(nx)], for_lower)
    sums = call(along_x_kernel, [((half, cols), bf16)] * (nx - 1), [], 10**9, *lower_pieces, *for_lower)
    summed_x = [send(sums[s - 1], "x", s) for s in range(1, nx)]
    for_upper = stage([(0, 0), (0, 1)], for_upper)
    sums = call(along_y_kernel, [((half, cols), bf16)], [], 10**9, *upper_pieces, *for_upper)
    summed_y = send(sums, "yh", 1)
    own = call(own_kernel, [((half, cols), f32)] * 2, [], 10**9, *upper_pieces, *for_upper, *lower_pieces, *for_lower)
    return call(finish_kernel, [((tokens, cols), bf16)], [], 0, *own, summed_y, *summed_x)


def solution(mesh):
    axes = Mesh(mesh.devices.reshape(8, 2, 2, 2, 4), ("z", "yl", "core", "yh", "x"))
    tp = ("yh", "x")
    placed = (P(CTX, None, tp), P(None, None, tp), P(None, tp + CTX), P(tp, None))
    return jax.shard_map(body, mesh=axes, in_specs=placed, out_specs=P(CTX, tp), check_vma=False)
```
